512 devices in a mesh: subj: 32 (over z, y_lo), slab: 16 (over y_hi, x, core).
Axes of the slice: x: 4, y: 8 (y_hi: 2, y_lo: 4; y = y_hi * 4 + y_lo), z: 8, core: 2. Of those that a mesh axis runs over, the one named last changes fastest.
Arguments:
- data_rhs: float32 [32, 16, 64, 1536], P('subj', None, 'slab'), may hold values from -12 to 12
- inv_var: float32 [32, 64, 1536], P('subj', 'slab'), may hold values from 0.01 to 0.3
- design: float32 [32, 16], P('subj'), may hold values from 0.5 to 4
- keep_mask: int32 [32, 64, 1536], P('subj', 'slab'), may hold values 0 or 1
- brain_mask: int32 [64, 1536], P('slab'), may hold values 0 or 1
- tissue: int32 [64, 1536], P('slab'), may hold values from 0 to 2
- kappa_sq: float32 [3, 16], replicated, may hold values from 0.005 to 0.5
- prior_scale: float32 [16], replicated, may hold values from 0.5 to 2
- mean_field: float32 [16, 64, 1536], P(None, 'slab', 'subj'), may hold values from -6 to 6
- pop_noise: float32 [16, 64, 1536], P(None, 'slab', 'subj'), may hold values from -6 to 6
Outputs:
- subject_fields: float32 [32, 16, 64, 1536], P('subj', None, 'slab')
- new_mean: float32 [16, 64, 1536], P(None, 'slab', 'subj')
The draws below stay inside these ranges and needn't reach their ends.
All inputs are finite; a program needn't handle non-finite values. No bound on the sum of `keep_mask` or of `brain_mask` on one device may be relied on, other than what follows from the above.
Results may differ from the reference program's by a relative error of at most 0.00016.
Values sent between devices are 32-bit elements; how exact they have to be, the bound alone decides.
A program may use at most 64 MiB of HBM per device.

```python
import math
import jax
import jax.numpy as jnp
from jax import lax

K = 16
CLASSES = 3
ITERS = 8
CX = 64
CY = 24
SUBJECTS = 32
NZ = 64


def touch_ends(values, stream_key, least, top_value):
    dims = values.shape
    index_at = [jax.random.randint(jax.random.fold_in(stream_key, axis), (), 0, dims[axis]) for axis in range(len(dims))]
    values = values.at[tuple(index_at)].set(least)
    longest = dims.index(max(dims))
    index_at[longest] = (index_at[longest] + 1) % dims[longest]
    return values.at[tuple(index_at)].set(top_value)


def with_spikes(result, rng, source, target, shards_of, factor):
    def block_of(dim):
        return (jnp.arange(result.shape[dim]) // (result.shape[dim] // shards_of)).reshape((-1,) + (1,) * (result.ndim - 1 - dim))

    near = jax.random.permutation(rng, shards_of)[block_of(target)]
    far = (block_of(target) + shards_of // 2) % shards_of
    return jnp.where((block_of(source) == near) | (block_of(source) == far), factor * result, result)


def block_levels(own_key, shape, split, low, top_value):
    factor_of = 1.0
    for dim, parts in split:
        heights = jax.random.uniform(jax.random.fold_in(jax.random.fold_in(own_key, 6), dim), (parts,), jnp.float32, low / len(split), top_value / len(split))
        factor_of = factor_of * jnp.repeat(jnp.exp(heights), shape[dim] // parts).reshape((-1,) + (1,) * (len(shape) - 1 - dim))
    return factor_of


def bell_draw(own_key, extent, width, reach, cuts=(), dtype=jnp.bfloat16):
    result = width * jax.random.normal(own_key, extent, jnp.float32)
    if cuts:
        result = result * block_levels(own_key, extent, cuts, -0.22, 0.18)
    return jnp.clip(result, -reach, reach).astype(dtype)


def heavy_noise(rng, dims, deviation, bound, pieces, heavy, held_as=jnp.bfloat16):
    values = deviation * jax.random.normal(rng, dims, jnp.float32)
    if pieces:
        values = values * block_levels(rng, dims, pieces, -0.22, 0.18)
    return jnp.clip(with_spikes(values, jax.random.fold_in(rng, 3), *heavy), -bound, bound).astype(held_as)


def setup_inputs(seed: int = 0) -> dict:
    keys = jax.random.split(jax.random.key(seed), 11)
    data_rhs = heavy_noise(keys[0], (SUBJECTS, K, NZ, CY * CX), 2.0, 12.0, ((0, 32), (2, 16)), (0, 3, 32, 2.75), jnp.float32)
    inv_var = jnp.clip(jnp.exp(math.log(0.3) - 3.4011974 * jax.random.uniform(keys[1], (SUBJECTS, NZ, CY * CX), jnp.float32) ** block_levels(keys[1], (SUBJECTS, NZ, CY * CX), ((0, 32), (1, 16)), -0.2, 0.2)), 0.01, 0.3)
    design = jnp.clip(jnp.exp(math.log(4.0) - 2.0794415 * jax.random.uniform(keys[2], (SUBJECTS, K), jnp.float32) ** block_levels(keys[2], (SUBJECTS, K), ((0, 32),), -0.2, 0.2)), 0.5, 4.0)
    keep_mask = touch_ends((jax.random.randint(keys[3], (SUBJECTS, NZ, CY * CX), 0, 10) < 9).astype(jnp.int32), jax.random.fold_in(keys[3], 1), 0, 1)
    brain_mask = touch_ends((jax.random.randint(keys[4], (NZ, CY * CX), 0, 5) < 4).astype(jnp.int32), jax.random.fold_in(keys[4], 1), 0, 1)
    tissue = touch_ends(jax.random.randint(keys[5], (NZ, CY * CX), 0, CLASSES), jax.random.fold_in(keys[5], 1), 0, CLASSES - 1).astype(jnp.int32)
    kappa_sq = jnp.clip(jnp.exp(jax.random.uniform(keys[6], (CLASSES, K), jnp.float32, math.log(0.005), math.log(0.5))), 0.005, 0.5)
    prior_scale = jnp.clip(jnp.exp(jax.random.uniform(keys[7], (K,), jnp.float32, math.log(0.5), math.log(2.0))), 0.5, 2.0)
    mean_field = bell_draw(keys[8], (K, NZ, CY * CX), 1.0, 6.0, ((1, 16), (2, 32)), jnp.float32)
    pop_noise = bell_draw(keys[9], (K, NZ, CY * CX), 1.0, 6.0, ((1, 16), (2, 32)), jnp.float32)
    return dict(data_rhs=data_rhs, inv_var=inv_var, design=design, keep_mask=keep_mask, brain_mask=brain_mask, tissue=tissue, kappa_sq=kappa_sq, prior_scale=prior_scale, mean_field=mean_field, pop_noise=pop_noise)


MEAN_PRECISION = 1.0

def prior_apply(values, kappa_field, prior_scale):
    regressors = values.shape[0]
    volume = values.reshape(regressors, NZ, CY, CX)
    padded = jnp.pad(volume, ((0, 0), (1, 1), (1, 1), (1, 1)))
    beside = padded[:, 2:, 1:-1, 1:-1] + padded[:, :-2, 1:-1, 1:-1]
    beside = beside + padded[:, 1:-1, 2:, 1:-1] + padded[:, 1:-1, :-2, 1:-1]
    beside = beside + padded[:, 1:-1, 1:-1, 2:] + padded[:, 1:-1, 1:-1, :-2]
    beside = beside.reshape(values.shape)
    return prior_scale[:, None, None] * ((6.0 + kappa_field) * values - beside)

def reference(data_rhs, inv_var, design, keep_mask, brain_mask, tissue, kappa_sq, prior_scale, mean_field, pop_noise):
    kappa_field = jnp.transpose(kappa_sq[tissue], (2, 0, 1))
    in_brain = brain_mask.astype(jnp.float32)
    prior_mean = prior_apply(mean_field, kappa_field, prior_scale)

    def solve_one(inputs):
        data_term, variance_inv, design_row, keep_row = inputs
        data_prec = design_row[:, None, None] * (variance_inv * in_brain * keep_row.astype(jnp.float32))[None]

        def operate(values):
            return data_prec * values + prior_apply(values, kappa_field, prior_scale)
        right_side = data_term + prior_mean
        solution = jnp.zeros_like(right_side)
        residual = right_side
        direction = right_side
        norm_now = lax.optimization_barrier(jnp.sum(residual * residual, axis=(1, 2)))
        for iteration in range(ITERS):
            applied = operate(direction)
            step_size = norm_now / lax.optimization_barrier(jnp.sum(direction * applied, axis=(1, 2)))
            solution = solution + step_size[:, None, None] * direction
            if iteration + 1 < ITERS:
                residual = residual - step_size[:, None, None] * applied
                norm_next = lax.optimization_barrier(jnp.sum(residual * residual, axis=(1, 2)))
                direction = residual + (norm_next / norm_now)[:, None, None] * direction
                norm_now = norm_next
        return solution
    fields_out = lax.map(solve_one, (data_rhs, inv_var, design, keep_mask))
    divisor = SUBJECTS + MEAN_PRECISION
    new_mean = lax.optimization_barrier(jnp.sum(fields_out, axis=0)) / divisor + pop_noise / math.sqrt(divisor)
    return (fields_out, new_mean)
```

```python
import math

import jax
import jax.numpy as jnp
from jax import lax
from jax.experimental import pallas as pl
from jax.experimental.pallas import tpu as pltpu
from jax.sharding import PartitionSpec as P

ITERS = 8
CX = 64
LANES = 128
MEAN_PRECISION = 1.0


def tiles_of(ref, row, columns):
    return [ref[row : row + 8, LANES * t : LANES * (t + 1)] for t in range(columns)]


def beside_tiles(ref, block, columns):
    lane = lax.broadcasted_iota(jnp.int32, (8, LANES), 1)
    column = lane % CX
    has_left = column > 0
    has_right = column < CX - 1
    low = lane < CX
    row = 8 + 8 * block
    center = tiles_of(ref, row, columns)
    before = tiles_of(ref, row - 1, columns)
    after = tiles_of(ref, row + 1, columns)
    swapped = [pltpu.roll(tile, CX, 1) for tile in center]
    zero = jnp.zeros((8, LANES), jnp.float32)
    sums = []
    for t in range(columns):
        left = jnp.where(has_left, pltpu.roll(center[t], 1, 1), 0.0)
        right = jnp.where(has_right, pltpu.roll(center[t], LANES - 1, 1), 0.0)
        prev_half = swapped[t - 1] if t else zero
        next_half = swapped[t + 1] if t + 1 < columns else zero
        rows = swapped[t] + jnp.where(low, prev_half, next_half)
        sums.append((left + right) + rows + (before[t] + after[t]))
    return center, sums


def total(parts):
    while len(parts) > 1:
        parts = [
            parts[i] + parts[i + 1] if i + 1 < len(parts) else parts[i]
            for i in range(0, len(parts), 2)
        ]
    return jnp.sum(parts[0], axis=(0, 1), keepdims=True)


def solve_kernel(
    design, kappa, scale_ref, rhs, factor, tissue, mean, out, direction, padded_mean, residual,
    applied, diagonal,
):
    regressor = lax.axis_index("slab")
    planes, cells = out.shape
    columns = cells // LANES
    blocks = planes // 8
    design_k = design[0, regressor]
    scale = scale_ref[regressor]
    edge = jnp.zeros((8, cells), jnp.float32)
    for ref in (direction, padded_mean):
        ref[0:8, :] = edge
        ref[8 + planes : 16 + planes, :] = edge
    padded_mean[8 : 8 + planes, :] = mean[...]
    norms = []
    for block in range(blocks):
        center, sums = beside_tiles(padded_mean, block, columns)
        for t in range(columns):
            at = (slice(8 * block, 8 * block + 8), slice(LANES * t, LANES * (t + 1)))
            label = tissue[at]
            kappa_field = jnp.where(
                label == 0,
                kappa[0, regressor],
                jnp.where(label == 1, kappa[1, regressor], kappa[2, regressor]),
            )
            shifted = 6.0 + kappa_field
            right_side = rhs[at] + scale * (shifted * center[t] - sums[t])
            diagonal[at] = design_k * factor[at] + scale * shifted
            residual[at] = right_side
            direction[8 + 8 * block : 16 + 8 * block, at[1]] = right_side
            norms.append(right_side * right_side)
        norms = [sum(norms[1:], norms[0])]
    out[...] = jnp.zeros((planes, cells), jnp.float32)

    def step(iteration, norm_now):
        curvs = []
        for block in range(blocks):
            center, sums = beside_tiles(direction, block, columns)
            for t in range(columns):
                at = (slice(8 * block, 8 * block + 8), slice(LANES * t, LANES * (t + 1)))
                value = diagonal[at] * center[t] - scale * sums[t]
                applied[at] = value
                curvs.append(center[t] * value)
            curvs = [total_tile(curvs)]
        step_size = norm_now / total(curvs)
        norms = []
        for block in range(blocks):
            for t in range(columns):
                at = (slice(8 * block, 8 * block + 8), slice(LANES * t, LANES * (t + 1)))
                out[at] += step_size * direction[8 + 8 * block : 16 + 8 * block, at[1]]
                value = residual[at] - step_size * applied[at]
                residual[at] = value
                norms.append(value * value)
            norms = [total_tile(norms)]
        norm_next = total(norms)
        ratio = norm_next / norm_now
        for block in range(blocks):
            for t in range(columns):
                at = (slice(8 * block, 8 * block + 8), slice(LANES * t, LANES * (t + 1)))
                own = (slice(8 + 8 * block, 16 + 8 * block), at[1])
                direction[own] = residual[at] + ratio * direction[own]
        return norm_next

    def last(norm_now):
        curvs = []
        for block in range(blocks):
            center, sums = beside_tiles(direction, block, columns)
            for t in range(columns):
                at = (slice(8 * block, 8 * block + 8), slice(LANES * t, LANES * (t + 1)))
                curvs.append(center[t] * (diagonal[at] * center[t] - scale * sums[t]))
            curvs = [total_tile(curvs)]
        step_size = norm_now / total(curvs)
        for block in range(blocks):
            for t in range(columns):
                at = (slice(8 * block, 8 * block + 8), slice(LANES * t, LANES * (t + 1)))
                out[at] += step_size * direction[8 + 8 * block : 16 + 8 * block, at[1]]

    last(lax.fori_loop(0, ITERS - 1, step, total(norms)))


def total_tile(parts):
    while len(parts) > 1:
        parts = [
            parts[i] + parts[i + 1] if i + 1 < len(parts) else parts[i]
            for i in range(0, len(parts), 2)
        ]
    return parts[0]


def solve(design, kappa_sq, prior_scale, rhs, factor, tissue, mean):
    planes, cells = rhs.shape
    vmem = pl.BlockSpec(memory_space=pltpu.VMEM)
    smem = pl.BlockSpec(memory_space=pltpu.SMEM)
    field = pltpu.VMEM((planes, cells), jnp.float32)
    padded = pltpu.VMEM((planes + 16, cells), jnp.float32)
    return pl.pallas_call(
        solve_kernel,
        out_shape=jax.ShapeDtypeStruct((planes, cells), jnp.float32),
        in_specs=[smem] * 3 + [vmem] * 4,
        out_specs=vmem,
        scratch_shapes=[padded, padded, field, field, field],
        name="solve",
    )(design, kappa_sq, prior_scale, rhs, factor, tissue, mean)


def local(
    data_rhs,
    inv_var,
    design,
    keep_mask,
    brain_mask,
    tissue,
    kappa_sq,
    prior_scale,
    mean_field,
    pop_noise,
):
    slabs = lax.axis_size("slab")
    depth, cells = tissue.shape
    planes = slabs * depth
    factor = inv_var[0] * (brain_mask.astype(jnp.float32) * keep_mask[0].astype(jnp.float32))
    sent = jnp.stack([factor, tissue.astype(jnp.float32)])
    both = lax.all_gather(sent, "slab", axis=1, tiled=True)
    rhs = lax.all_to_all(data_rhs[0], "slab", 0, 0, tiled=True).reshape(planes, cells)
    mean = lax.all_to_all(mean_field, "slab", 0, 0, tiled=True).reshape(planes, -1)
    mean = lax.all_gather(mean, "subj", axis=1, tiled=True)
    fields = solve(design, kappa_sq, prior_scale, rhs, both[0], both[1], mean)
    back = lax.all_to_all(fields.reshape(slabs, depth, cells), "slab", 0, 0, tiled=True)
    summed = lax.psum_scatter(fields, "subj", scatter_dimension=1, tiled=True)
    summed = lax.all_to_all(summed.reshape(slabs, depth, -1), "slab", 0, 0, tiled=True)
    divisor = lax.axis_size("subj") + MEAN_PRECISION
    new_mean = summed / divisor + pop_noise / math.sqrt(divisor)
    return (back[None], new_mean)


def solution(mesh):
    in_specs = (
        P("subj", None, "slab", None),
        P("subj", "slab", None),
        P("subj", None),
        P("subj", "slab", None),
        P("slab", None),
        P("slab", None),
        P(),
        P(),
        P(None, "slab", "subj"),
        P(None, "slab", "subj"),
    )
    out_specs = (P("subj", None, "slab", None), P(None, "slab", "subj"))
    return jax.shard_map(local, mesh=mesh, in_specs=in_specs, out_specs=out_specs, check_vma=False)
```

```python
import math

import jax
import jax.numpy as jnp
from jax import lax
from jax.experimental import pallas as pl
from jax.experimental.pallas import tpu as pltpu
from jax.sharding import PartitionSpec as P

ITERS = 8
CX = 64
LANES = 128
MEAN_PRECISION = 1.0


def tiles_of(ref, row, columns):
    return [ref[row : row + 8, LANES * t : LANES * (t + 1)] for t in range(columns)]


def beside_tiles(ref, block, columns):
    lane = lax.broadcasted_iota(jnp.int32, (8, LANES), 1)
    column = lane % CX
    has_left = column > 0
    has_right = column < CX - 1
    low = lane < CX
    row = 8 + 8 * block
    center = tiles_of(ref, row, columns)
    before = tiles_of(ref, row - 1, columns)
    after = tiles_of(ref, row + 1, columns)
    swapped = [pltpu.roll(tile, CX, 1) for tile in center]
    zero = jnp.zeros((8, LANES), jnp.float32)
    sums = []
    for t in range(columns):
        left = jnp.where(has_left, pltpu.roll(center[t], 1, 1), 0.0)
        right = jnp.where(has_right, pltpu.roll(center[t], LANES - 1, 1), 0.0)
        prev_half = swapped[t - 1] if t else zero
        next_half = swapped[t + 1] if t + 1 < columns else zero
        rows = swapped[t] + jnp.where(low, prev_half, next_half)
        sums.append((left + right) + rows + (before[t] + after[t]))
    return center, sums


def total(parts):
    while len(parts) > 1:
        parts = [
            parts[i] + parts[i + 1] if i + 1 < len(parts) else parts[i]
            for i in range(0, len(parts), 2)
        ]
    return jnp.sum(parts[0], axis=(0, 1), keepdims=True)


def unpack_pieces(pieces, padded):
    count, half, _ = pieces.shape
    cells = padded.shape[1]
    width = cells // count
    lane = lax.broadcasted_iota(jnp.int32, (half, LANES), 1)
    for upper in range(2):
        for t in range(cells // LANES):
            value = None
            first = LANES * t // width
            for piece in range(first, (LANES * (t + 1) - 1) // width + 1):
                start = piece * width - LANES * t
                moved = pieces[piece]
                turn = (start - upper * width) % LANES
                if turn:
                    moved = pltpu.roll(moved, turn, 1)
                value = moved if value is None else jnp.where(lane >= start, moved, value)
            padded[8 + upper * half : 8 + (upper + 1) * half, LANES * t : LANES * (t + 1)] = value


def pack_pieces(fields, pieces):
    count, half, _ = pieces.shape
    cells = fields.shape[1]
    width = cells // count
    lane = lax.broadcasted_iota(jnp.int32, (half, LANES), 1)
    for piece in range(count):
        t, offset = divmod(piece * width, LANES)
        sides = []
        for upper in range(2):
            turn = (upper * width - offset) % LANES
            value = None
            for source in range(t, (piece * width + width - 1) // LANES + 1):
                tile = fields[half * upper : half * (upper + 1), LANES * source : LANES * (source + 1)]
                moved = pltpu.roll(tile, turn, 1) if turn else tile
                if value is None:
                    value = moved
                else:
                    value = jnp.where(lane < LANES - offset + upper * width, value, moved)
            sides.append(value)
        pieces[piece] = jnp.where(lane < width, sides[0], sides[1])


def solve_kernel(
    design, kappa, scale_ref, rhs, factor, tissue, mean, out, pieces, direction, padded_mean,
    residual, applied, diagonal,
):
    regressor = lax.axis_index("slab")
    planes, cells = out.shape
    columns = cells // LANES
    blocks = planes // 8
    design_k = design[0, regressor]
    scale = scale_ref[regressor]
    edge = jnp.zeros((8, cells), jnp.float32)
    for ref in (direction, padded_mean):
        ref[0:8, :] = edge
        ref[8 + planes : 16 + planes, :] = edge
    unpack_pieces(mean, padded_mean)
    norms = []
    for block in range(blocks):
        center, sums = beside_tiles(padded_mean, block, columns)
        for t in range(columns):
            at = (slice(8 * block, 8 * block + 8), slice(LANES * t, LANES * (t + 1)))
            label = tissue[at]
            kappa_field = jnp.where(
                label == 0,
                kappa[0, regressor],
                jnp.where(label == 1, kappa[1, regressor], kappa[2, regressor]),
            )
            shifted = 6.0 + kappa_field
            right_side = rhs[at] + scale * (shifted * center[t] - sums[t])
            diagonal[at] = design_k * factor[at] + scale * shifted
            residual[at] = right_side
            direction[8 + 8 * block : 16 + 8 * block, at[1]] = right_side
            norms.append(right_side * right_side)
        norms = [sum(norms[1:], norms[0])]
    out[...] = jnp.zeros((planes, cells), jnp.float32)

    def step(iteration, norm_now):
        curvs = []
        for block in range(blocks):
            center, sums = beside_tiles(direction, block, columns)
            for t in range(columns):
                at = (slice(8 * block, 8 * block + 8), slice(LANES * t, LANES * (t + 1)))
                value = diagonal[at] * center[t] - scale * sums[t]
                applied[at] = value
                curvs.append(center[t] * value)
            curvs = [total_tile(curvs)]
        step_size = norm_now / total(curvs)
        norms = []
        for block in range(blocks):
            for t in range(columns):
                at = (slice(8 * block, 8 * block + 8), slice(LANES * t, LANES * (t + 1)))
                out[at] += step_size * direction[8 + 8 * block : 16 + 8 * block, at[1]]
                value = residual[at] - step_size * applied[at]
                residual[at] = value
                norms.append(value * value)
            norms = [total_tile(norms)]
        norm_next = total(norms)
        ratio = norm_next / norm_now
        for block in range(blocks):
            for t in range(columns):
                at = (slice(8 * block, 8 * block + 8), slice(LANES * t, LANES * (t + 1)))
                own = (slice(8 + 8 * block, 16 + 8 * block), at[1])
                direction[own] = residual[at] + ratio * direction[own]
        return norm_next

    def last(norm_now):
        curvs = []
        for block in range(blocks):
            center, sums = beside_tiles(direction, block, columns)
            for t in range(columns):
                at = (slice(8 * block, 8 * block + 8), slice(LANES * t, LANES * (t + 1)))
                curvs.append(center[t] * (diagonal[at] * center[t] - scale * sums[t]))
            curvs = [total_tile(curvs)]
        step_size = norm_now / total(curvs)
        for block in range(blocks):
            for t in range(columns):
                at = (slice(8 * block, 8 * block + 8), slice(LANES * t, LANES * (t + 1)))
                out[at] += step_size * direction[8 + 8 * block : 16 + 8 * block, at[1]]

    last(lax.fori_loop(0, ITERS - 1, step, total(norms)))
    pack_pieces(out, pieces)


def total_tile(parts):
    while len(parts) > 1:
        parts = [
            parts[i] + parts[i + 1] if i + 1 < len(parts) else parts[i]
            for i in range(0, len(parts), 2)
        ]
    return parts[0]


def solve(design, kappa_sq, prior_scale, rhs, factor, tissue, mean):
    planes, cells = rhs.shape
    vmem = pl.BlockSpec(memory_space=pltpu.VMEM)
    smem = pl.BlockSpec(memory_space=pltpu.SMEM)
    field = pltpu.VMEM((planes, cells), jnp.float32)
    padded = pltpu.VMEM((planes + 16, cells), jnp.float32)
    return pl.pallas_call(
        solve_kernel,
        out_shape=[
            jax.ShapeDtypeStruct((planes, cells), jnp.float32),
            jax.ShapeDtypeStruct(mean.shape, jnp.float32),
        ],
        in_specs=[smem] * 3 + [vmem] * 4,
        out_specs=[vmem, vmem],
        scratch_shapes=[padded, padded, field, field, field],
        name="solve",
    )(design, kappa_sq, prior_scale, rhs, factor, tissue, mean)


def local(
    data_rhs,
    inv_var,
    design,
    keep_mask,
    brain_mask,
    tissue,
    kappa_sq,
    prior_scale,
    mean_field,
    pop_noise,
):
    slabs, subjects = lax.axis_size("slab"), lax.axis_size("subj")
    depth, cells = tissue.shape
    planes = slabs * depth
    width = cells // subjects
    half = planes // 2

    def exchange(values, axis):
        return lax.all_to_all(values, axis, 0, 0, tiled=True)

    def gather(values, axis):
        return exchange(jnp.broadcast_to(values, (lax.axis_size(axis),) + values.shape), axis)

    mean = exchange(mean_field, "slab").reshape(2, half, width)
    spare = jnp.zeros((half, LANES - 2 * width), jnp.float32)
    mean = gather(jnp.concatenate([mean[0], mean[1], spare], axis=1), "subj")
    rhs = exchange(data_rhs[0], "slab").reshape(planes, cells)
    factor = inv_var[0] * (brain_mask.astype(jnp.float32) * keep_mask[0].astype(jnp.float32))
    factor = gather(factor, "slab").reshape(planes, cells)
    label = gather(tissue.astype(jnp.float32), "slab").reshape(planes, cells)
    fields, pieces = solve(design, kappa_sq, prior_scale, rhs, factor, label, mean)
    summed = jnp.sum(exchange(pieces, "subj"), axis=0)
    summed = jnp.concatenate([summed[:, :width], summed[:, width : 2 * width]], axis=0)
    summed = exchange(summed.reshape(slabs, depth, width), "slab")
    back = exchange(fields.reshape(slabs, depth, cells), "slab")
    divisor = subjects + MEAN_PRECISION
    new_mean = summed / divisor + pop_noise / math.sqrt(divisor)
    return (back[None], new_mean)


def solution(mesh):
    in_specs = (
        P("subj", None, "slab", None),
        P("subj", "slab", None),
        P("subj", None),
        P("subj", "slab", None),
        P("slab", None),
        P("slab", None),
        P(),
        P(),
        P(None, "slab", "subj"),
        P(None, "slab", "subj"),
    )
    out_specs = (P("subj", None, "slab", None), P(None, "slab", "subj"))
    return jax.shard_map(local, mesh=mesh, in_specs=in_specs, out_specs=out_specs, check_vma=False)
```

```python
import math

import jax
import jax.numpy as jnp
from jax import lax
from jax.experimental import pallas as pl
from jax.experimental.pallas import tpu as pltpu
from jax.sharding import PartitionSpec as P

ITERS = 8
CX = 64
LANES = 128
MEAN_PRECISION = 1.0


def tiles_of(ref, row, columns):
    return [ref[row : row + 8, LANES * t : LANES * (t + 1)] for t in range(columns)]


def beside_tiles(ref, block, columns):
    lane = lax.broadcasted_iota(jnp.int32, (8, LANES), 1)
    column = lane % CX
    has_left = column > 0
    has_right = column < CX - 1
    low = lane < CX
    row = 8 + 8 * block
    center = tiles_of(ref, row, columns)
    before = tiles_of(ref, row - 1, columns)
    after = tiles_of(ref, row + 1, columns)
    swapped = [pltpu.roll(tile, CX, 1) for tile in center]
    zero = jnp.zeros((8, LANES), jnp.float32)
    sums = []
    for t in range(columns):
        left = jnp.where(has_left, pltpu.roll(center[t], 1, 1), 0.0)
        right = jnp.where(has_right, pltpu.roll(center[t], LANES - 1, 1), 0.0)
        prev_half = swapped[t - 1] if t else zero
        next_half = swapped[t + 1] if t + 1 < columns else zero
        rows = swapped[t] + jnp.where(low, prev_half, next_half)
        sums.append((left + right) + rows + (before[t] + after[t]))
    return center, sums


def total(parts):
    while len(parts) > 1:
        parts = [
            parts[i] + parts[i + 1] if i + 1 < len(parts) else parts[i]
            for i in range(0, len(parts), 2)
        ]
    return jnp.sum(parts[0], axis=(0, 1), keepdims=True)


def unpack_pieces(pieces, padded):
    count, half, _ = pieces.shape
    cells = padded.shape[1]
    width = cells // count
    lane = lax.broadcasted_iota(jnp.int32, (half, LANES), 1)
    for upper in range(2):
        for t in range(cells // LANES):
            value = None
            first = LANES * t // width
            for piece in range(first, (LANES * (t + 1) - 1) // width + 1):
                start = piece * width - LANES * t
                moved = pieces[piece]
                turn = (start - upper * width) % LANES
                if turn:
                    moved = pltpu.roll(moved, turn, 1)
                value = moved if value is None else jnp.where(lane >= start, moved, value)
            for pair in range(half // 2):
                row = 8 + 4 * pair + 2 * upper
                padded[row : row + 2, LANES * t : LANES * (t + 1)] = value[2 * pair : 2 * pair + 2]


def pack_pieces(fields, pieces, halves):
    count, half, _ = pieces.shape
    cells = fields.shape[1]
    width = cells // count
    lane = lax.broadcasted_iota(jnp.int32, (half, LANES), 1)
    for upper in range(2):
        for pair in range(half // 2):
            row = 4 * pair + 2 * upper
            halves[upper, 2 * pair : 2 * pair + 2, :] = fields[row : row + 2, :]
    for piece in range(count):
        t, offset = divmod(piece * width, LANES)
        sides = []
        for upper in range(2):
            turn = (upper * width - offset) % LANES
            value = None
            for source in range(t, (piece * width + width - 1) // LANES + 1):
                tile = halves[upper, :, LANES * source : LANES * (source + 1)]
                moved = pltpu.roll(tile, turn, 1) if turn else tile
                if value is None:
                    value = moved
                else:
                    value = jnp.where(lane < LANES - offset + upper * width, value, moved)
            sides.append(value)
        pieces[piece] = jnp.where(lane < width, sides[0], sides[1])


def solve_kernel(
    design, kappa, scale_ref, rhs, both, mean, slab_fields, pieces, direction, padded_mean, residual,
    applied, diagonal, out, halves,
):
    regressor = lax.axis_index("slab")
    planes, cells = out.shape
    columns = cells // LANES
    blocks = planes // 8
    design_k = design[0, regressor]
    scale = scale_ref[regressor]
    edge = jnp.zeros((8, cells), jnp.float32)
    for ref in (direction, padded_mean):
        ref[0:8, :] = edge
        ref[8 + planes : 16 + planes, :] = edge
    unpack_pieces(mean, padded_mean)
    depth = planes // rhs.shape[0]
    for slab in range(rhs.shape[0]):
        rows = slice(depth * slab, depth * (slab + 1))
        residual[rows, :] = rhs[slab]
        diagonal[rows, :] = both[slab, 0]
        applied[rows, :] = both[slab, 1]
    norms = []
    for block in range(blocks):
        center, sums = beside_tiles(padded_mean, block, columns)
        for t in range(columns):
            at = (slice(8 * block, 8 * block + 8), slice(LANES * t, LANES * (t + 1)))
            label = applied[at]
            kappa_field = jnp.where(
                label == 0,
                kappa[0, regressor],
                jnp.where(label == 1, kappa[1, regressor], kappa[2, regressor]),
            )
            shifted = 6.0 + kappa_field
            right_side = residual[at] + scale * (shifted * center[t] - sums[t])
            diagonal[at] = design_k * diagonal[at] + scale * shifted
            residual[at] = right_side
            direction[8 + 8 * block : 16 + 8 * block, at[1]] = right_side
            norms.append(right_side * right_side)
        norms = [sum(norms[1:], norms[0])]
    out[...] = jnp.zeros((planes, cells), jnp.float32)

    def step(iteration, norm_now):
        curvs = []
        for block in range(blocks):
            center, sums = beside_tiles(direction, block, columns)
            for t in range(columns):
                at = (slice(8 * block, 8 * block + 8), slice(LANES * t, LANES * (t + 1)))
                value = diagonal[at] * center[t] - scale * sums[t]
                applied[at] = value
                curvs.append(center[t] * value)
            curvs = [total_tile(curvs)]
        step_size = norm_now / total(curvs)
        norms = []
        for block in range(blocks):
            for t in range(columns):
                at = (slice(8 * block, 8 * block + 8), slice(LANES * t, LANES * (t + 1)))
                out[at] += step_size * direction[8 + 8 * block : 16 + 8 * block, at[1]]
                value = residual[at] - step_size * applied[at]
                residual[at] = value
                norms.append(value * value)
            norms = [total_tile(norms)]
        norm_next = total(norms)
        ratio = norm_next / norm_now
        for block in range(blocks):
            for t in range(columns):
                at = (slice(8 * block, 8 * block + 8), slice(LANES * t, LANES * (t + 1)))
                own = (slice(8 + 8 * block, 16 + 8 * block), at[1])
                direction[own] = residual[at] + ratio * direction[own]
        return norm_next

    def last(norm_now):
        curvs = []
        for block in range(blocks):
            center, sums = beside_tiles(direction, block, columns)
            for t in range(columns):
                at = (slice(8 * block, 8 * block + 8), slice(LANES * t, LANES * (t + 1)))
                curvs.append(center[t] * (diagonal[at] * center[t] - scale * sums[t]))
            curvs = [total_tile(curvs)]
        step_size = norm_now / total(curvs)
        for block in range(blocks):
            for t in range(columns):
                at = (slice(8 * block, 8 * block + 8), slice(LANES * t, LANES * (t + 1)))
                out[at] += step_size * direction[8 + 8 * block : 16 + 8 * block, at[1]]

    last(lax.fori_loop(0, ITERS - 1, step, total(norms)))
    for slab in range(rhs.shape[0]):
        slab_fields[slab] = out[depth * slab : depth * (slab + 1), :]
    pack_pieces(out, pieces, halves)


def total_tile(parts):
    while len(parts) > 1:
        parts = [
            parts[i] + parts[i + 1] if i + 1 < len(parts) else parts[i]
            for i in range(0, len(parts), 2)
        ]
    return parts[0]


def solve(design, kappa_sq, prior_scale, rhs, both, mean):
    slabs, depth, cells = rhs.shape
    planes = slabs * depth
    vmem = pl.BlockSpec(memory_space=pltpu.VMEM)
    smem = pl.BlockSpec(memory_space=pltpu.SMEM)
    field = pltpu.VMEM((planes, cells), jnp.float32)
    padded = pltpu.VMEM((planes + 16, cells), jnp.float32)
    halves = pltpu.VMEM((2, planes // 2, cells), jnp.float32)
    return pl.pallas_call(
        solve_kernel,
        out_shape=[
            jax.ShapeDtypeStruct(rhs.shape, jnp.float32),
            jax.ShapeDtypeStruct(mean.shape, jnp.float32),
        ],
        in_specs=[smem] * 3 + [vmem] * 3,
        out_specs=[vmem, vmem],
        scratch_shapes=[padded, padded, field, field, field, field, halves],
        name="solve",
    )(design, kappa_sq, prior_scale, rhs, both, mean)


def greet(axes):
    barrier = pltpu.get_barrier_semaphore()
    peers = 0
    for axis in axes:
        size, me = lax.axis_size(axis), lax.axis_index(axis)

        def signal(offset, carry):
            pl.semaphore_signal(
                barrier,
                inc=1,
                device_id={axis: lax.rem(me + offset, size)},
                device_id_type=pl.DeviceIdType.MESH,
            )
            return carry

        lax.fori_loop(1, size, signal, 0)
        peers += size - 1
    pl.semaphore_wait(barrier, peers)


class Exchange:
    def __init__(self, source, target, axis, sems, whole=False):
        self.size, self.me = lax.axis_size(axis), lax.axis_index(axis)
        self.source, self.target, self.axis, self.whole = source, target, axis, whole
        self.send, self.receive, self.own = sems

    def block(self, index):
        return self.source if self.whole else self.source.at[index]

    def remote(self, offset):
        to = lax.rem(self.me + offset, self.size)
        return pltpu.make_async_remote_copy(
            src_ref=self.block(to),
            dst_ref=self.target.at[self.me],
            send_sem=self.send.at[offset - 1],
            recv_sem=self.receive.at[offset - 1],
            device_id={self.axis: to},
            device_id_type=pl.DeviceIdType.MESH,
        )

    def local(self):
        return pltpu.make_async_copy(self.block(self.me), self.target.at[self.me], self.own)

    def start(self):
        def one(offset, carry):
            self.remote(offset).start()
            return carry

        lax.fori_loop(1, self.size, one, 0)
        self.local().start()

    def wait(self):
        def one(offset, carry):
            self.remote(offset).wait()
            return carry

        self.local().wait()
        lax.fori_loop(1, self.size, one, 0)


def exchange_sems(axis):
    count = lax.axis_size(axis) - 1
    return [
        pltpu.SemaphoreType.DMA((count,)),
        pltpu.SemaphoreType.DMA((count,)),
        pltpu.SemaphoreType.DMA,
    ]


def bring_kernel(rhs, both, mean, rhs_out, both_out, mean_out, held, *sems):
    small = Exchange(mean, held, "slab", sems[0:3])
    spread = Exchange(held, mean_out, "subj", sems[3:6], whole=True)
    large = Exchange(rhs, rhs_out, "slab", sems[6:9])
    shared = Exchange(both, both_out, "slab", sems[9:12], whole=True)
    greet(("slab", "subj"))
    small.start()
    large.start()
    shared.start()
    small.wait()
    spread.start()
    large.wait()
    shared.wait()
    spread.wait()


def bring(rhs, both, mean):
    slabs, subjects = lax.axis_size("slab"), lax.axis_size("subj")
    vmem = pl.BlockSpec(memory_space=pltpu.VMEM)
    return pl.pallas_call(
        bring_kernel,
        out_shape=[
            jax.ShapeDtypeStruct(rhs.shape, jnp.float32),
            jax.ShapeDtypeStruct((slabs,) + both.shape, jnp.float32),
            jax.ShapeDtypeStruct((subjects,) + mean.shape, jnp.float32),
        ],
        in_specs=[vmem] * 3,
        out_specs=[vmem] * 3,
        scratch_shapes=[
            pltpu.VMEM(mean.shape, jnp.float32),
            *exchange_sems("slab"),
            *exchange_sems("subj"),
            *exchange_sems("slab"),
            *exchange_sems("slab"),
        ],
        compiler_params=pltpu.CompilerParams(collective_id=0, has_side_effects=True),
        name="bring",
    )(rhs, both, mean)


def give_kernel(fields, pieces, fields_out, mean_out, arrived, summed, *sems):
    parts = Exchange(pieces, arrived, "subj", sems[0:3])
    large = Exchange(fields, fields_out, "slab", sems[3:6])
    small = Exchange(summed, mean_out, "slab", sems[6:9])
    greet(("slab", "subj"))
    parts.start()
    large.start()
    parts.wait()
    summed[...] = jnp.sum(arrived[...], axis=0)
    small.start()
    large.wait()
    small.wait()


def give(fields, pieces):
    slabs = lax.axis_size("slab")
    vmem = pl.BlockSpec(memory_space=pltpu.VMEM)
    small = (slabs,) + pieces.shape[2:]
    return pl.pallas_call(
        give_kernel,
        out_shape=[
            jax.ShapeDtypeStruct(fields.shape, jnp.float32),
            jax.ShapeDtypeStruct(small, jnp.float32),
        ],
        in_specs=[vmem] * 2,
        out_specs=[vmem] * 2,
        scratch_shapes=[
            pltpu.VMEM(pieces.shape, jnp.float32),
            pltpu.VMEM(small, jnp.float32),
            *exchange_sems("subj"),
            *exchange_sems("slab"),
            *exchange_sems("slab"),
        ],
        compiler_params=pltpu.CompilerParams(collective_id=1, has_side_effects=True),
        name="give",
    )(fields, pieces)


def local(
    data_rhs,
    inv_var,
    design,
    keep_mask,
    brain_mask,
    tissue,
    kappa_sq,
    prior_scale,
    mean_field,
    pop_noise,
):
    slabs, subjects = lax.axis_size("slab"), lax.axis_size("subj")
    depth, cells = tissue.shape
    width = cells // subjects
    pair = depth // 2
    spare = jnp.zeros((slabs, pair, LANES - 2 * width), jnp.float32)
    mean = jnp.concatenate([mean_field[:, :pair], mean_field[:, pair:], spare], axis=2)
    factor = inv_var[0] * (brain_mask.astype(jnp.float32) * keep_mask[0].astype(jnp.float32))
    both = jnp.stack([factor, tissue.astype(jnp.float32)])
    rhs, both, mean = bring(data_rhs[0], both, mean)
    mean = mean.reshape(subjects, slabs * pair, LANES)
    fields, pieces = solve(design, kappa_sq, prior_scale, rhs, both, mean)
    back, summed = give(fields, pieces.reshape(subjects, slabs, pair, LANES))
    summed = jnp.concatenate([summed[..., :width], summed[..., width : 2 * width]], axis=1)
    divisor = subjects + MEAN_PRECISION
    new_mean = summed / divisor + pop_noise / math.sqrt(divisor)
    return (back[None], new_mean)


def solution(mesh):
    in_specs = (
        P("subj", None, "slab", None),
        P("subj", "slab", None),
        P("subj", None),
        P("subj", "slab", None),
        P("slab", None),
        P("slab", None),
        P(),
        P(),
        P(None, "slab", "subj"),
        P(None, "slab", "subj"),
    )
    out_specs = (P("subj", None, "slab", None), P(None, "slab", "subj"))
    return jax.shard_map(local, mesh=mesh, in_specs=in_specs, out_specs=out_specs, check_vma=False)
```

```python
import math

import jax
import jax.numpy as jnp
from jax import lax
from jax.experimental import pallas as pl
from jax.experimental.pallas import tpu as pltpu
from jax.sharding import PartitionSpec as P

ITERS = 8
CX = 64
LANES = 128
MEAN_PRECISION = 1.0
CORES = 2
ROW = 4


def tiles_of(ref, row, columns):
    return [ref[row : row + 8, LANES * t : LANES * (t + 1)] for t in range(columns)]


def beside_tiles(ref, block, columns):
    lane = lax.broadcasted_iota(jnp.int32, (8, LANES), 1)
    column = lane % CX
    has_left = column > 0
    has_right = column < CX - 1
    low = lane < CX
    row = 8 + 8 * block
    center = tiles_of(ref, row, columns)
    before = tiles_of(ref, row - 1, columns)
    after = tiles_of(ref, row + 1, columns)
    swapped = [pltpu.roll(tile, CX, 1) for tile in center]
    zero = jnp.zeros((8, LANES), jnp.float32)
    sums = []
    for t in range(columns):
        left = jnp.where(has_left, pltpu.roll(center[t], 1, 1), 0.0)
        right = jnp.where(has_right, pltpu.roll(center[t], LANES - 1, 1), 0.0)
        prev_half = swapped[t - 1] if t else zero
        next_half = swapped[t + 1] if t + 1 < columns else zero
        rows = swapped[t] + jnp.where(low, prev_half, next_half)
        sums.append((left + right) + rows + (before[t] + after[t]))
    return center, sums


def total(parts):
    while len(parts) > 1:
        parts = [
            parts[i] + parts[i + 1] if i + 1 < len(parts) else parts[i]
            for i in range(0, len(parts), 2)
        ]
    return jnp.sum(parts[0], axis=(0, 1), keepdims=True)


def unpack_pieces(pieces, padded):
    count, half, _ = pieces.shape
    cells = padded.shape[1]
    width = cells // count
    lane = lax.broadcasted_iota(jnp.int32, (half, LANES), 1)
    for upper in range(2):
        for t in range(cells // LANES):
            value = None
            first = LANES * t // width
            for piece in range(first, (LANES * (t + 1) - 1) // width + 1):
                start = piece * width - LANES * t
                moved = pieces[piece]
                turn = (start - upper * width) % LANES
                if turn:
                    moved = pltpu.roll(moved, turn, 1)
                value = moved if value is None else jnp.where(lane >= start, moved, value)
            for pair in range(half // 2):
                row = 8 + 4 * pair + 2 * upper
                padded[row : row + 2, LANES * t : LANES * (t + 1)] = value[2 * pair : 2 * pair + 2]


def pack_pieces(fields, pieces, halves):
    count, half, _ = pieces.shape
    cells = fields.shape[1]
    width = cells // count
    lane = lax.broadcasted_iota(jnp.int32, (half, LANES), 1)
    for upper in range(2):
        for pair in range(half // 2):
            row = 4 * pair + 2 * upper
            halves[upper, 2 * pair : 2 * pair + 2, :] = fields[row : row + 2, :]
    for piece in range(count):
        t, offset = divmod(piece * width, LANES)
        sides = []
        for upper in range(2):
            turn = (upper * width - offset) % LANES
            value = None
            for source in range(t, (piece * width + width - 1) // LANES + 1):
                tile = halves[upper, :, LANES * source : LANES * (source + 1)]
                moved = pltpu.roll(tile, turn, 1) if turn else tile
                if value is None:
                    value = moved
                else:
                    value = jnp.where(lane < LANES - offset + upper * width, value, moved)
            sides.append(value)
        pieces[piece] = jnp.where(lane < width, sides[0], sides[1])


def solve_kernel(
    design, kappa, scale_ref, rhs, both, mean, slab_fields, pieces, direction, padded_mean, residual,
    applied, diagonal, out, halves,
):
    regressor = lax.axis_index("slab")
    planes, cells = out.shape
    columns = cells // LANES
    blocks = planes // 8
    design_k = design[0, regressor]
    scale = scale_ref[regressor]
    edge = jnp.zeros((8, cells), jnp.float32)
    for ref in (direction, padded_mean):
        ref[0:8, :] = edge
        ref[8 + planes : 16 + planes, :] = edge
    unpack_pieces(mean, padded_mean)
    depth = planes // rhs.shape[0]
    for slab in range(rhs.shape[0]):
        rows = slice(depth * slab, depth * (slab + 1))
        residual[rows, :] = rhs[slab]
        diagonal[rows, :] = both[slab, 0]
        applied[rows, :] = both[slab, 1]
    norms = []
    for block in range(blocks):
        center, sums = beside_tiles(padded_mean, block, columns)
        for t in range(columns):
            at = (slice(8 * block, 8 * block + 8), slice(LANES * t, LANES * (t + 1)))
            label = applied[at]
            kappa_field = jnp.where(
                label == 0,
                kappa[0, regressor],
                jnp.where(label == 1, kappa[1, regressor], kappa[2, regressor]),
            )
            shifted = 6.0 + kappa_field
            right_side = residual[at] + scale * (shifted * center[t] - sums[t])
            diagonal[at] = design_k * diagonal[at] + scale * shifted
            residual[at] = right_side
            direction[8 + 8 * block : 16 + 8 * block, at[1]] = right_side
            norms.append(right_side * right_side)
        norms = [sum(norms[1:], norms[0])]
    out[...] = jnp.zeros((planes, cells), jnp.float32)

    def step(iteration, norm_now):
        curvs = []
        for block in range(blocks):
            center, sums = beside_tiles(direction, block, columns)
            for t in range(columns):
                at = (slice(8 * block, 8 * block + 8), slice(LANES * t, LANES * (t + 1)))
                value = diagonal[at] * center[t] - scale * sums[t]
                applied[at] = value
                curvs.append(center[t] * value)
            curvs = [total_tile(curvs)]
        step_size = norm_now / total(curvs)
        norms = []
        for block in range(blocks):
            for t in range(columns):
                at = (slice(8 * block, 8 * block + 8), slice(LANES * t, LANES * (t + 1)))
                out[at] += step_size * direction[8 + 8 * block : 16 + 8 * block, at[1]]
                value = residual[at] - step_size * applied[at]
                residual[at] = value
                norms.append(value * value)
            norms = [total_tile(norms)]
        norm_next = total(norms)
        ratio = norm_next / norm_now
        for block in range(blocks):
            for t in range(columns):
                at = (slice(8 * block, 8 * block + 8), slice(LANES * t, LANES * (t + 1)))
                own = (slice(8 + 8 * block, 16 + 8 * block), at[1])
                direction[own] = residual[at] + ratio * direction[own]
        return norm_next

    def last(norm_now):
        curvs = []
        for block in range(blocks):
            center, sums = beside_tiles(direction, block, columns)
            for t in range(columns):
                at = (slice(8 * block, 8 * block + 8), slice(LANES * t, LANES * (t + 1)))
                curvs.append(center[t] * (diagonal[at] * center[t] - scale * sums[t]))
            curvs = [total_tile(curvs)]
        step_size = norm_now / total(curvs)
        for block in range(blocks):
            for t in range(columns):
                at = (slice(8 * block, 8 * block + 8), slice(LANES * t, LANES * (t + 1)))
                out[at] += step_size * direction[8 + 8 * block : 16 + 8 * block, at[1]]

    last(lax.fori_loop(0, ITERS - 1, step, total(norms)))
    for slab in range(rhs.shape[0]):
        slab_fields[slab] = out[depth * slab : depth * (slab + 1), :]
    pack_pieces(out, pieces, halves)


def total_tile(parts):
    while len(parts) > 1:
        parts = [
            parts[i] + parts[i + 1] if i + 1 < len(parts) else parts[i]
            for i in range(0, len(parts), 2)
        ]
    return parts[0]


def solve(design, kappa_sq, prior_scale, rhs, both, mean):
    slabs, depth, cells = rhs.shape
    planes = slabs * depth
    vmem = pl.BlockSpec(memory_space=pltpu.VMEM)
    smem = pl.BlockSpec(memory_space=pltpu.SMEM)
    field = pltpu.VMEM((planes, cells), jnp.float32)
    padded = pltpu.VMEM((planes + 16, cells), jnp.float32)
    halves = pltpu.VMEM((2, planes // 2, cells), jnp.float32)
    return pl.pallas_call(
        solve_kernel,
        out_shape=[
            jax.ShapeDtypeStruct(rhs.shape, jnp.float32),
            jax.ShapeDtypeStruct(mean.shape, jnp.float32),
        ],
        in_specs=[smem] * 3 + [vmem] * 3,
        out_specs=[vmem, vmem],
        scratch_shapes=[padded, padded, field, field, field, field, halves],
        name="solve",
    )(design, kappa_sq, prior_scale, rhs, both, mean)


def ring(axis, stride, count):
    index = lax.axis_index(axis)
    place = lax.rem(lax.div(index, stride), count)
    return axis, count - 1, lambda i: index + (lax.rem(place + i + 1, count) - place) * stride


def across(axis, low):
    index = lax.axis_index(axis)
    place = lax.rem(index, low)
    base = index - place
    other = lax.rem(base + low, 2 * low)
    return axis, low, lambda i: other + lax.rem(place + i, low)


def greet(*groups):
    barrier = pltpu.get_barrier_semaphore()
    for axis, count, peer in groups:

        def signal(i, carry):
            pl.semaphore_signal(
                barrier, inc=1, device_id={axis: peer(i)}, device_id_type=pl.DeviceIdType.MESH
            )
            return carry

        lax.fori_loop(0, count, signal, 0)
    pl.semaphore_wait(barrier, sum(count for _, count, _ in groups))


class Exchange:
    def __init__(self, group, source, target, sems):
        self.axis, self.count, self.peer = group
        self.source, self.target = source, target
        self.send, self.receive = sems

    def remote(self, i):
        to = self.peer(i)
        return pltpu.make_async_remote_copy(
            src_ref=self.source(i, to),
            dst_ref=self.target(i),
            send_sem=self.send.at[i],
            recv_sem=self.receive.at[i],
            device_id={self.axis: to},
            device_id_type=pl.DeviceIdType.MESH,
        )

    def start(self):
        def one(i, carry):
            self.remote(i).start()
            return carry

        lax.fori_loop(0, self.count, one, 0)

    def wait(self):
        def one(i, carry):
            self.remote(i).wait()
            return carry

        lax.fori_loop(0, self.count, one, 0)


def exchange_sems(*counts):
    return [pltpu.SemaphoreType.DMA((count,)) for count in counts for _ in range(2)]


def bring_kernel(rhs, both, mean, rhs_out, both_out, mean_out, held, own, *sems):
    slabs, subjects = rhs.shape[0], mean_out.shape[0]
    slab, subject = lax.axis_index("slab"), lax.axis_index("subj")
    half = slabs // 2
    mirror = lax.rem(slab + half, slabs)
    core = lax.rem(slab, CORES)
    layer = pl.ds(subject - lax.rem(subject, ROW), ROW)
    near = ring("slab", 1, half)
    far = across("slab", half)
    along_x = ring("slab", CORES, half // CORES)
    along_y = ring("subj", 1, ROW)
    along_z = ring("subj", ROW, subjects // ROW)
    partner = ring("slab", 1, CORES)[2](0)

    def pair(k):
        return sems[2 * k], sems[2 * k + 1]

    def take(ref):
        return lambda i, to: ref.at[to]

    def put(ref, index):
        return lambda i: ref.at[index]

    small_near = Exchange(near, take(mean), put(held, slab), pair(0))
    small_far = Exchange(far, take(mean), put(held, slab), pair(1))
    large_near = Exchange(near, take(rhs), put(rhs_out, slab), pair(2))
    large_far = Exchange(far, take(rhs), put(rhs_out, slab), pair(3))
    over = Exchange(
        ("slab", 1, lambda i: mirror), lambda i, to: both, put(both_out, slab), pair(4)
    )
    beside = Exchange(along_x, lambda i, to: both, put(both_out, slab), pair(5))
    passed = Exchange(
        along_x, lambda i, to: both_out.at[mirror], put(both_out, mirror), pair(6)
    )
    twin = Exchange(
        ("slab", half, lambda i: partner),
        lambda i, to: both_out.at[CORES * i + core],
        lambda i: both_out.at[CORES * i + core],
        pair(7),
    )
    row = Exchange(along_y, lambda i, to: held, put(mean_out, subject), pair(8))
    column = Exchange(
        along_z, lambda i, to: mean_out.at[layer], lambda i: mean_out.at[layer], pair(9)
    )
    kept = [
        pltpu.make_async_copy(mean.at[slab], held.at[slab], own.at[0]),
        pltpu.make_async_copy(rhs.at[slab], rhs_out.at[slab], own.at[1]),
        pltpu.make_async_copy(both, both_out.at[slab], own.at[2]),
        pltpu.make_async_copy(held, mean_out.at[subject], own.at[3]),
    ]
    greet(near, far, along_y, along_z)
    small_far.start()
    small_near.start()
    over.start()
    beside.start()
    large_near.start()
    for copy in kept[:3]:
        copy.start()
    kept[0].wait()
    small_near.wait()
    small_far.wait()
    row.start()
    kept[3].start()
    large_far.start()
    over.wait()
    passed.start()
    kept[3].wait()
    row.wait()
    column.start()
    kept[2].wait()
    beside.wait()
    passed.wait()
    twin.start()
    kept[1].wait()
    large_near.wait()
    twin.wait()
    large_far.wait()
    column.wait()


def bring(rhs, both, mean):
    slabs, subjects = lax.axis_size("slab"), lax.axis_size("subj")
    half = slabs // 2
    x_peers = half // CORES - 1
    vmem = pl.BlockSpec(memory_space=pltpu.VMEM)
    return pl.pallas_call(
        bring_kernel,
        out_shape=[
            jax.ShapeDtypeStruct(rhs.shape, jnp.float32),
            jax.ShapeDtypeStruct((slabs,) + both.shape, jnp.float32),
            jax.ShapeDtypeStruct((subjects,) + mean.shape, jnp.float32),
        ],
        in_specs=[vmem] * 3,
        out_specs=[vmem] * 3,
        scratch_shapes=[
            pltpu.VMEM(mean.shape, jnp.float32),
            pltpu.SemaphoreType.DMA((4,)),
            *exchange_sems(half - 1, half, half - 1, half, 1, x_peers, x_peers, half),
            *exchange_sems(ROW - 1, subjects // ROW - 1),
        ],
        compiler_params=pltpu.CompilerParams(collective_id=0, has_side_effects=True),
        name="bring",
    )(rhs, both, mean)


def give_kernel(
    fields, pieces, fields_out, mean_out, layers, partial, rows, summed, own, *sems
):
    slabs, subjects = fields.shape[0], pieces.shape[0]
    slab, subject = lax.axis_index("slab"), lax.axis_index("subj")
    half = slabs // 2
    y = lax.rem(subject, ROW)
    z = lax.div(subject, ROW)
    near = ring("slab", 1, half)
    far = across("slab", half)
    along_y = ring("subj", 1, ROW)
    along_z = ring("subj", ROW, subjects // ROW)

    def pair(k):
        return sems[2 * k], sems[2 * k + 1]

    def take(ref):
        return lambda i, to: ref.at[to]

    def put(ref, index):
        return lambda i: ref.at[index]

    column = Exchange(
        along_z, lambda i, to: pieces.at[pl.ds(to - y, ROW)], put(layers, z), pair(0)
    )
    row = Exchange(
        along_y, lambda i, to: partial.at[lax.rem(to, ROW)], put(rows, y), pair(1)
    )
    large_far = Exchange(far, take(fields), put(fields_out, slab), pair(2))
    large_near = Exchange(near, take(fields), put(fields_out, slab), pair(3))
    small_far = Exchange(far, take(summed), put(mean_out, slab), pair(4))
    small_near = Exchange(near, take(summed), put(mean_out, slab), pair(5))
    kept = [
        pltpu.make_async_copy(pieces.at[pl.ds(subject - y, ROW)], layers.at[z], own.at[0]),
        pltpu.make_async_copy(partial.at[y], rows.at[y], own.at[1]),
        pltpu.make_async_copy(fields.at[slab], fields_out.at[slab], own.at[2]),
        pltpu.make_async_copy(summed.at[slab], mean_out.at[slab], own.at[3]),
    ]
    greet(near, far, along_y, along_z)
    column.start()
    large_far.start()
    large_near.start()
    kept[0].start()
    kept[2].start()
    kept[0].wait()
    column.wait()
    partial[...] = jnp.sum(layers[...], axis=0)
    row.start()
    kept[1].start()
    kept[1].wait()
    row.wait()
    summed[...] = jnp.sum(rows[...], axis=0)
    small_far.start()
    small_near.start()
    kept[3].start()
    for copy in kept[2:]:
        copy.wait()
    for exchange in (large_near, large_far, small_near, small_far):
        exchange.wait()


def give(fields, pieces):
    slabs, subjects = lax.axis_size("slab"), lax.axis_size("subj")
    half, depth = slabs // 2, subjects // ROW
    vmem = pl.BlockSpec(memory_space=pltpu.VMEM)
    small = pieces.shape[1:]
    return pl.pallas_call(
        give_kernel,
        out_shape=[
            jax.ShapeDtypeStruct(fields.shape, jnp.float32),
            jax.ShapeDtypeStruct(small, jnp.float32),
        ],
        in_specs=[vmem] * 2,
        out_specs=[vmem] * 2,
        scratch_shapes=[
            pltpu.VMEM((depth, ROW) + small, jnp.float32),
            pltpu.VMEM((ROW,) + small, jnp.float32),
            pltpu.VMEM((ROW,) + small, jnp.float32),
            pltpu.VMEM(small, jnp.float32),
            pltpu.SemaphoreType.DMA((4,)),
            *exchange_sems(depth - 1, ROW - 1, half, half - 1, half, half - 1),
        ],
        compiler_params=pltpu.CompilerParams(collective_id=1, has_side_effects=True),
        name="give",
    )(fields, pieces)


def local(
    data_rhs,
    inv_var,
    design,
    keep_mask,
    brain_mask,
    tissue,
    kappa_sq,
    prior_scale,
    mean_field,
    pop_noise,
):
    slabs, subjects = lax.axis_size("slab"), lax.axis_size("subj")
    depth, cells = tissue.shape
    width = cells // subjects
    pair = depth // 2
    spare = jnp.zeros((slabs, pair, LANES - 2 * width), jnp.float32)
    mean = jnp.concatenate([mean_field[:, :pair], mean_field[:, pair:], spare], axis=2)
    factor = inv_var[0] * (brain_mask.astype(jnp.float32) * keep_mask[0].astype(jnp.float32))
    both = jnp.stack([factor, tissue.astype(jnp.float32)])
    rhs, both, mean = bring(data_rhs[0], both, mean)
    mean = mean.reshape(subjects, slabs * pair, LANES)
    fields, pieces = solve(design, kappa_sq, prior_scale, rhs, both, mean)
    back, summed = give(fields, pieces.reshape(subjects, slabs, pair, LANES))
    summed = jnp.concatenate([summed[..., :width], summed[..., width : 2 * width]], axis=1)
    divisor = subjects + MEAN_PRECISION
    new_mean = summed / divisor + pop_noise / math.sqrt(divisor)
    return (back[None], new_mean)


def solution(mesh):
    in_specs = (
        P("subj", None, "slab", None),
        P("subj", "slab", None),
        P("subj", None),
        P("subj", "slab", None),
        P("slab", None),
        P("slab", None),
        P(),
        P(),
        P(None, "slab", "subj"),
        P(None, "slab", "subj"),
    )
    out_specs = (P("subj", None, "slab", None), P(None, "slab", "subj"))
    return jax.shard_map(local, mesh=mesh, in_specs=in_specs, out_specs=out_specs, check_vma=False)
```

```python
import math

import jax
import jax.numpy as jnp
from jax import lax
from jax.experimental import pallas as pl
from jax.experimental.pallas import tpu as pltpu
from jax.sharding import PartitionSpec as P

ITERS = 8
CX = 64
LANES = 128
MEAN_PRECISION = 1.0
CORES = 2
ROW = 4


def tiles_of(ref, row, columns):
    return [ref[row : row + 8, LANES * t : LANES * (t + 1)] for t in range(columns)]


def beside_tiles(ref, block, columns):
    lane = lax.broadcasted_iota(jnp.int32, (8, LANES), 1)
    column = lane % CX
    has_left = column > 0
    has_right = column < CX - 1
    low = lane < CX
    row = 8 + 8 * block
    center = tiles_of(ref, row, columns)
    before = tiles_of(ref, row - 1, columns)
    after = tiles_of(ref, row + 1, columns)
    swapped = [pltpu.roll(tile, CX, 1) for tile in center]
    zero = jnp.zeros((8, LANES), jnp.float32)
    sums = []
    for t in range(columns):
        left = jnp.where(has_left, pltpu.roll(center[t], 1, 1), 0.0)
        right = jnp.where(has_right, pltpu.roll(center[t], LANES - 1, 1), 0.0)
        prev_half = swapped[t - 1] if t else zero
        next_half = swapped[t + 1] if t + 1 < columns else zero
        rows = swapped[t] + jnp.where(low, prev_half, next_half)
        sums.append((left + right) + rows + (before[t] + after[t]))
    return center, sums


def total(parts):
    while len(parts) > 1:
        parts = [
            parts[i] + parts[i + 1] if i + 1 < len(parts) else parts[i]
            for i in range(0, len(parts), 2)
        ]
    return jnp.sum(parts[0], axis=(0, 1), keepdims=True)


def unpack_pieces(pieces, padded):
    count, half, _ = pieces.shape
    cells = padded.shape[1]
    width = cells // count
    lane = lax.broadcasted_iota(jnp.int32, (half, LANES), 1)
    for upper in range(2):
        for t in range(cells // LANES):
            value = None
            first = LANES * t // width
            for piece in range(first, (LANES * (t + 1) - 1) // width + 1):
                start = piece * width - LANES * t
                moved = pieces[piece]
                turn = (start - upper * width) % LANES
                if turn:
                    moved = pltpu.roll(moved, turn, 1)
                value = moved if value is None else jnp.where(lane >= start, moved, value)
            for pair in range(half // 2):
                row = 8 + 4 * pair + 2 * upper
                padded[row : row + 2, LANES * t : LANES * (t + 1)] = value[2 * pair : 2 * pair + 2]


def pack_pieces(fields, pieces, halves):
    count, half, _ = pieces.shape
    cells = fields.shape[1]
    width = cells // count
    lane = lax.broadcasted_iota(jnp.int32, (half, LANES), 1)
    for upper in range(2):
        for pair in range(half // 2):
            row = 4 * pair + 2 * upper
            halves[upper, 2 * pair : 2 * pair + 2, :] = fields[row : row + 2, :]
    for piece in range(count):
        t, offset = divmod(piece * width, LANES)
        sides = []
        for upper in range(2):
            turn = (upper * width - offset) % LANES
            value = None
            for source in range(t, (piece * width + width - 1) // LANES + 1):
                tile = halves[upper, :, LANES * source : LANES * (source + 1)]
                moved = pltpu.roll(tile, turn, 1) if turn else tile
                if value is None:
                    value = moved
                else:
                    value = jnp.where(lane < LANES - offset + upper * width, value, moved)
            sides.append(value)
        pieces[piece] = jnp.where(lane < width, sides[0], sides[1])


def solve_kernel(
    design, kappa, scale_ref, rhs, both, mean, slab_fields, pieces, direction, padded_mean, residual,
    applied, diagonal, out, halves,
):
    regressor = lax.axis_index("slab")
    planes, cells = out.shape
    columns = cells // LANES
    blocks = planes // 8
    design_k = design[0, regressor]
    scale = scale_ref[regressor]
    edge = jnp.zeros((8, cells), jnp.float32)
    for ref in (direction, padded_mean):
        ref[0:8, :] = edge
        ref[8 + planes : 16 + planes, :] = edge
    unpack_pieces(mean, padded_mean)
    depth = planes // rhs.shape[0]
    for slab in range(rhs.shape[0]):
        rows = slice(depth * slab, depth * (slab + 1))
        residual[rows, :] = rhs[slab]
        diagonal[rows, :] = both[slab, 0]
        applied[rows, :] = both[slab, 1]
    norms = []
    for block in range(blocks):
        center, sums = beside_tiles(padded_mean, block, columns)
        for t in range(columns):
            at = (slice(8 * block, 8 * block + 8), slice(LANES * t, LANES * (t + 1)))
            label = applied[at]
            kappa_field = jnp.where(
                label == 0,
                kappa[0, regressor],
                jnp.where(label == 1, kappa[1, regressor], kappa[2, regressor]),
            )
            shifted = 6.0 + kappa_field
            right_side = residual[at] + scale * (shifted * center[t] - sums[t])
            diagonal[at] = design_k * diagonal[at] + scale * shifted
            residual[at] = right_side
            direction[8 + 8 * block : 16 + 8 * block, at[1]] = right_side
            norms.append(right_side * right_side)
        norms = [sum(norms[1:], norms[0])]
    out[...] = jnp.zeros((planes, cells), jnp.float32)

    def step(iteration, norm_now):
        curvs = []
        for block in range(blocks):
            center, sums = beside_tiles(direction, block, columns)
            for t in range(columns):
                at = (slice(8 * block, 8 * block + 8), slice(LANES * t, LANES * (t + 1)))
                value = diagonal[at] * center[t] - scale * sums[t]
                applied[at] = value
                curvs.append(center[t] * value)
            curvs = [total_tile(curvs)]
        step_size = norm_now / total(curvs)
        norms = []
        for block in range(blocks):
            for t in range(columns):
                at = (slice(8 * block, 8 * block + 8), slice(LANES * t, LANES * (t + 1)))
                out[at] += step_size * direction[8 + 8 * block : 16 + 8 * block, at[1]]
                value = residual[at] - step_size * applied[at]
                residual[at] = value
                norms.append(value * value)
            norms = [total_tile(norms)]
        norm_next = total(norms)
        ratio = norm_next / norm_now
        for block in range(blocks):
            for t in range(columns):
                at = (slice(8 * block, 8 * block + 8), slice(LANES * t, LANES * (t + 1)))
                own = (slice(8 + 8 * block, 16 + 8 * block), at[1])
                direction[own] = residual[at] + ratio * direction[own]
        return norm_next

    def last(norm_now):
        curvs = []
        for block in range(blocks):
            center, sums = beside_tiles(direction, block, columns)
            for t in range(columns):
                at = (slice(8 * block, 8 * block + 8), slice(LANES * t, LANES * (t + 1)))
                curvs.append(center[t] * (diagonal[at] * center[t] - scale * sums[t]))
            curvs = [total_tile(curvs)]
        step_size = norm_now / total(curvs)
        for block in range(blocks):
            for t in range(columns):
                at = (slice(8 * block, 8 * block + 8), slice(LANES * t, LANES * (t + 1)))
                out[at] += step_size * direction[8 + 8 * block : 16 + 8 * block, at[1]]

    last(lax.fori_loop(0, ITERS - 1, step, total(norms)))
    for slab in range(rhs.shape[0]):
        slab_fields[slab] = out[depth * slab : depth * (slab + 1), :]
    pack_pieces(out, pieces, halves)


def total_tile(parts):
    while len(parts) > 1:
        parts = [
            parts[i] + parts[i + 1] if i + 1 < len(parts) else parts[i]
            for i in range(0, len(parts), 2)
        ]
    return parts[0]


def solve(design, kappa_sq, prior_scale, rhs, both, mean):
    slabs, depth, cells = rhs.shape
    planes = slabs * depth
    vmem = pl.BlockSpec(memory_space=pltpu.VMEM)
    smem = pl.BlockSpec(memory_space=pltpu.SMEM)
    field = pltpu.VMEM((planes, cells), jnp.float32)
    padded = pltpu.VMEM((planes + 16, cells), jnp.float32)
    halves = pltpu.VMEM((2, planes // 2, cells), jnp.float32)
    return pl.pallas_call(
        solve_kernel,
        out_shape=[
            jax.ShapeDtypeStruct(rhs.shape, jnp.float32),
            jax.ShapeDtypeStruct(mean.shape, jnp.float32),
        ],
        in_specs=[smem] * 3 + [vmem] * 3,
        out_specs=[vmem, vmem],
        scratch_shapes=[padded, padded, field, field, field, field, halves],
        name="solve",
    )(design, kappa_sq, prior_scale, rhs, both, mean)


def ring(axis, stride, count):
    index = lax.axis_index(axis)
    place = lax.rem(lax.div(index, stride), count)
    return axis, count - 1, lambda i: index + (lax.rem(place + i + 1, count) - place) * stride


def farthest_first(group):
    axis, peers, peer = group
    middle = (peers + 1) // 2 - 1

    def ordered(i):
        return peer(middle + lax.div(i + 1, 2) * (2 * lax.rem(i, 2) - 1))

    return axis, peers, ordered


def across(axis, low, first, count):
    index = lax.axis_index(axis)
    place = lax.rem(index, low)
    base = index - place
    other = lax.rem(base + low, 2 * low)
    return axis, count, lambda i: other + lax.rem(place + first + i, low)


def greet(*groups):
    barrier = pltpu.get_barrier_semaphore()
    for axis, count, peer in groups:

        def signal(i, carry):
            pl.semaphore_signal(
                barrier, inc=1, device_id={axis: peer(i)}, device_id_type=pl.DeviceIdType.MESH
            )
            return carry

        lax.fori_loop(0, count, signal, 0)
    pl.semaphore_wait(barrier, sum(count for _, count, _ in groups))


class Exchange:
    def __init__(self, group, source, target, sems):
        self.axis, self.count, self.peer = group
        self.source, self.target = source, target
        self.send, self.receive = sems

    def remote(self, i):
        to = self.peer(i)
        return pltpu.make_async_remote_copy(
            src_ref=self.source(i, to),
            dst_ref=self.target(i),
            send_sem=self.send.at[i],
            recv_sem=self.receive.at[i],
            device_id={self.axis: to},
            device_id_type=pl.DeviceIdType.MESH,
        )

    def start(self):
        def one(i, carry):
            self.remote(i).start()
            return carry

        lax.fori_loop(0, self.count, one, 0)

    def wait(self):
        def one(i, carry):
            self.remote(i).wait()
            return carry

        lax.fori_loop(0, self.count, one, 0)


def exchange_sems(*counts):
    return [pltpu.SemaphoreType.DMA((count,)) for count in counts for _ in range(2)]


def bring_kernel(rhs, both, mean, rhs_out, both_out, mean_out, held, own, *sems):
    slabs, subjects = rhs.shape[0], mean_out.shape[0]
    slab, subject = lax.axis_index("slab"), lax.axis_index("subj")
    half = slabs // 2
    mirror = lax.rem(slab + half, slabs)
    core = lax.rem(slab, CORES)
    near = ring("slab", 1, half)
    far = across("slab", half, 0, half)
    early = across("slab", half, 0, half // 2)
    late = across("slab", half, half // 2, half - half // 2)
    along_x = ring("slab", CORES, half // CORES)
    along_y = ring("subj", 1, ROW)
    depth = subjects // ROW
    along_z = ring("subj", ROW, depth)
    up, down = depth // 2, depth - 1 - depth // 2
    above, below = along_z[2](0), along_z[2](depth - 2)
    z = lax.div(subject, ROW)
    partner = ring("slab", 1, CORES)[2](0)

    def pair(k):
        return sems[2 * k], sems[2 * k + 1]

    def take(ref):
        return lambda i, to: ref.at[to]

    def put(ref, index):
        return lambda i: ref.at[index]

    small_near = Exchange(near, take(mean), put(held, slab), pair(0))
    small_far = Exchange(far, take(mean), put(held, slab), pair(1))
    large_near = Exchange(near, take(rhs), put(rhs_out, slab), pair(2))
    large_early = Exchange(early, take(rhs), put(rhs_out, slab), pair(3))
    large_late = Exchange(late, take(rhs), put(rhs_out, slab), pair(9))
    over = Exchange(
        ("slab", 1, lambda i: mirror), lambda i, to: both, put(both_out, slab), pair(4)
    )
    beside = Exchange(along_x, lambda i, to: both, put(both_out, slab), pair(5))
    passed = Exchange(
        along_x, lambda i, to: both_out.at[mirror], put(both_out, mirror), pair(6)
    )
    twin = Exchange(
        ("slab", half, lambda i: partner),
        lambda i, to: both_out.at[CORES * i + core],
        lambda i: both_out.at[CORES * i + core],
        pair(7),
    )
    row = Exchange(along_y, lambda i, to: held, put(mean_out, subject), pair(8))

    def hop(to, distance, k):
        layer = mean_out.at[pl.ds(ROW * lax.rem(z + depth + distance, depth), ROW)]
        return Exchange(("subj", 1, lambda i: to), lambda i, _: layer, lambda i: layer, pair(k))

    ups = [hop(above, -step, 10 + step) for step in range(up)]
    downs = [hop(below, step, 10 + up + step) for step in range(down)]

    def onward(step):
        for hops in (ups, downs):
            if step < len(hops):
                hops[step - 1].wait()
                hops[step].start()

    kept = [
        pltpu.make_async_copy(mean.at[slab], held.at[slab], own.at[0]),
        pltpu.make_async_copy(rhs.at[slab], rhs_out.at[slab], own.at[1]),
        pltpu.make_async_copy(both, both_out.at[slab], own.at[2]),
        pltpu.make_async_copy(held, mean_out.at[subject], own.at[3]),
    ]
    greet(near, far, along_y, along_z)
    small_far.start()
    small_near.start()
    over.start()
    beside.start()
    large_early.start()
    large_near.start()
    for copy in kept[:3]:
        copy.start()
    kept[0].wait()
    small_near.wait()
    small_far.wait()
    row.start()
    kept[3].start()
    large_late.start()
    over.wait()
    passed.start()
    kept[3].wait()
    row.wait()
    ups[0].start()
    downs[0].start()
    onward(1)
    kept[2].wait()
    beside.wait()
    passed.wait()
    twin.start()
    for step in range(2, max(up, down)):
        onward(step)
    kept[1].wait()
    large_near.wait()
    twin.wait()
    large_early.wait()
    large_late.wait()
    ups[-1].wait()
    downs[-1].wait()


def bring(rhs, both, mean):
    slabs, subjects = lax.axis_size("slab"), lax.axis_size("subj")
    half = slabs // 2
    x_peers = half // CORES - 1
    vmem = pl.BlockSpec(memory_space=pltpu.VMEM)
    return pl.pallas_call(
        bring_kernel,
        out_shape=[
            jax.ShapeDtypeStruct(rhs.shape, jnp.float32),
            jax.ShapeDtypeStruct((slabs,) + both.shape, jnp.float32),
            jax.ShapeDtypeStruct((subjects,) + mean.shape, jnp.float32),
        ],
        in_specs=[vmem] * 3,
        out_specs=[vmem] * 3,
        scratch_shapes=[
            pltpu.VMEM(mean.shape, jnp.float32),
            pltpu.SemaphoreType.DMA((4,)),
            *exchange_sems(half - 1, half, half - 1, half // 2, 1, x_peers, x_peers, half),
            *exchange_sems(ROW - 1, half - half // 2, *[1] * (subjects // ROW - 1)),
        ],
        compiler_params=pltpu.CompilerParams(collective_id=0, has_side_effects=True),
        name="bring",
    )(rhs, both, mean)


def give_kernel(
    fields, pieces, fields_out, mean_out, layers, partial, rows, summed, own, *sems
):
    slabs, subjects = fields.shape[0], pieces.shape[0]
    slab, subject = lax.axis_index("slab"), lax.axis_index("subj")
    half = slabs // 2
    y = lax.rem(subject, ROW)
    z = lax.div(subject, ROW)
    near = ring("slab", 1, half)
    far = across("slab", half, 0, half)
    along_y = ring("subj", 1, ROW)
    along_z = farthest_first(ring("subj", ROW, subjects // ROW))

    def pair(k):
        return sems[2 * k], sems[2 * k + 1]

    def take(ref):
        return lambda i, to: ref.at[to]

    def put(ref, index):
        return lambda i: ref.at[index]

    column = Exchange(
        along_z, lambda i, to: pieces.at[pl.ds(to - y, ROW)], put(layers, z), pair(0)
    )
    row = Exchange(
        along_y, lambda i, to: partial.at[lax.rem(to, ROW)], put(rows, y), pair(1)
    )
    large_far = Exchange(far, take(fields), put(fields_out, slab), pair(2))
    large_near = Exchange(near, take(fields), put(fields_out, slab), pair(3))
    small_far = Exchange(far, take(summed), put(mean_out, slab), pair(4))
    small_near = Exchange(near, take(summed), put(mean_out, slab), pair(5))
    kept = [
        pltpu.make_async_copy(pieces.at[pl.ds(subject - y, ROW)], layers.at[z], own.at[0]),
        pltpu.make_async_copy(partial.at[y], rows.at[y], own.at[1]),
        pltpu.make_async_copy(fields.at[slab], fields_out.at[slab], own.at[2]),
        pltpu.make_async_copy(summed.at[slab], mean_out.at[slab], own.at[3]),
    ]
    greet(near, far, along_y, along_z)
    column.start()
    large_far.start()
    large_near.start()
    kept[0].start()
    kept[2].start()
    kept[0].wait()
    column.wait()
    partial[...] = jnp.sum(layers[...], axis=0)
    row.start()
    kept[1].start()
    kept[1].wait()
    row.wait()
    summed[...] = jnp.sum(rows[...], axis=0)
    small_far.start()
    small_near.start()
    kept[3].start()
    for copy in kept[2:]:
        copy.wait()
    for exchange in (large_near, large_far, small_near, small_far):
        exchange.wait()


def give(fields, pieces):
    slabs, subjects = lax.axis_size("slab"), lax.axis_size("subj")
    half, depth = slabs // 2, subjects // ROW
    vmem = pl.BlockSpec(memory_space=pltpu.VMEM)
    small = pieces.shape[1:]
    return pl.pallas_call(
        give_kernel,
        out_shape=[
            jax.ShapeDtypeStruct(fields.shape, jnp.float32),
            jax.ShapeDtypeStruct(small, jnp.float32),
        ],
        in_specs=[vmem] * 2,
        out_specs=[vmem] * 2,
        scratch_shapes=[
            pltpu.VMEM((depth, ROW) + small, jnp.float32),
            pltpu.VMEM((ROW,) + small, jnp.float32),
            pltpu.VMEM((ROW,) + small, jnp.float32),
            pltpu.VMEM(small, jnp.float32),
            pltpu.SemaphoreType.DMA((4,)),
            *exchange_sems(depth - 1, ROW - 1, half, half - 1, half, half - 1),
        ],
        compiler_params=pltpu.CompilerParams(collective_id=1, has_side_effects=True),
        name="give",
    )(fields, pieces)


def local(
    data_rhs,
    inv_var,
    design,
    keep_mask,
    brain_mask,
    tissue,
    kappa_sq,
    prior_scale,
    mean_field,
    pop_noise,
):
    slabs, subjects = lax.axis_size("slab"), lax.axis_size("subj")
    depth, cells = tissue.shape
    width = cells // subjects
    pair = depth // 2
    spare = jnp.zeros((slabs, pair, LANES - 2 * width), jnp.float32)
    mean = jnp.concatenate([mean_field[:, :pair], mean_field[:, pair:], spare], axis=2)
    factor = inv_var[0] * (brain_mask.astype(jnp.float32) * keep_mask[0].astype(jnp.float32))
    both = jnp.stack([factor, tissue.astype(jnp.float32)])
    rhs, both, mean = bring(data_rhs[0], both, mean)
    mean = mean.reshape(subjects, slabs * pair, LANES)
    fields, pieces = solve(design, kappa_sq, prior_scale, rhs, both, mean)
    back, summed = give(fields, pieces.reshape(subjects, slabs, pair, LANES))
    summed = jnp.concatenate([summed[..., :width], summed[..., width : 2 * width]], axis=1)
    divisor = subjects + MEAN_PRECISION
    new_mean = summed / divisor + pop_noise / math.sqrt(divisor)
    return (back[None], new_mean)


def solution(mesh):
    in_specs = (
        P("subj", None, "slab", None),
        P("subj", "slab", None),
        P("subj", None),
        P("subj", "slab", None),
        P("slab", None),
        P("slab", None),
        P(),
        P(),
        P(None, "slab", "subj"),
        P(None, "slab", "subj"),
    )
    out_specs = (P("subj", None, "slab", None), P(None, "slab", "subj"))
    return jax.shard_map(local, mesh=mesh, in_specs=in_specs, out_specs=out_specs, check_vma=False)
```

```python
import math

import jax
import jax.numpy as jnp
from jax import lax
from jax.experimental import pallas as pl
from jax.experimental.pallas import tpu as pltpu
from jax.sharding import PartitionSpec as P

ITERS = 8
CX = 64
LANES = 128
MEAN_PRECISION = 1.0
CORES = 2
ROW = 4


def tiles_of(ref, row, columns):
    return [ref[row : row + 8, LANES * t : LANES * (t + 1)] for t in range(columns)]


def beside_tiles(ref, block, columns):
    lane = lax.broadcasted_iota(jnp.int32, (8, LANES), 1)
    column = lane % CX
    has_left = column > 0
    has_right = column < CX - 1
    low = lane < CX
    row = 8 + 8 * block
    center = tiles_of(ref, row, columns)
    before = tiles_of(ref, row - 1, columns)
    after = tiles_of(ref, row + 1, columns)
    swapped = [pltpu.roll(tile, CX, 1) for tile in center]
    zero = jnp.zeros((8, LANES), jnp.float32)
    sums = []
    for t in range(columns):
        left = jnp.where(has_left, pltpu.roll(center[t], 1, 1), 0.0)
        right = jnp.where(has_right, pltpu.roll(center[t], LANES - 1, 1), 0.0)
        prev_half = swapped[t - 1] if t else zero
        next_half = swapped[t + 1] if t + 1 < columns else zero
        rows = swapped[t] + jnp.where(low, prev_half, next_half)
        sums.append((left + right) + rows + (before[t] + after[t]))
    return center, sums


def total(parts):
    while len(parts) > 1:
        parts = [
            parts[i] + parts[i + 1] if i + 1 < len(parts) else parts[i]
            for i in range(0, len(parts), 2)
        ]
    return jnp.sum(parts[0], axis=(0, 1), keepdims=True)


def unpack_pieces(pieces, padded):
    count, half, _ = pieces.shape
    cells = padded.shape[1]
    width = cells // count
    lane = lax.broadcasted_iota(jnp.int32, (half, LANES), 1)
    for upper in range(2):
        for t in range(cells // LANES):
            value = None
            first = LANES * t // width
            for piece in range(first, (LANES * (t + 1) - 1) // width + 1):
                start = piece * width - LANES * t
                moved = pieces[piece]
                turn = (start - upper * width) % LANES
                if turn:
                    moved = pltpu.roll(moved, turn, 1)
                value = moved if value is None else jnp.where(lane >= start, moved, value)
            for pair in range(half // 2):
                row = 8 + 4 * pair + 2 * upper
                padded[row : row + 2, LANES * t : LANES * (t + 1)] = value[2 * pair : 2 * pair + 2]


def pack_pieces(fields, pieces, halves):
    count, half, _ = pieces.shape
    cells = fields.shape[1]
    width = cells // count
    lane = lax.broadcasted_iota(jnp.int32, (half, LANES), 1)
    for upper in range(2):
        for pair in range(half // 2):
            row = 4 * pair + 2 * upper
            halves[upper, 2 * pair : 2 * pair + 2, :] = fields[row : row + 2, :]
    for piece in range(count):
        t, offset = divmod(piece * width, LANES)
        sides = []
        for upper in range(2):
            turn = (upper * width - offset) % LANES
            value = None
            for source in range(t, (piece * width + width - 1) // LANES + 1):
                tile = halves[upper, :, LANES * source : LANES * (source + 1)]
                moved = pltpu.roll(tile, turn, 1) if turn else tile
                if value is None:
                    value = moved
                else:
                    value = jnp.where(lane < LANES - offset + upper * width, value, moved)
            sides.append(value)
        pieces[piece] = jnp.where(lane < width, sides[0], sides[1])


def solve_kernel(
    design, kappa, scale_ref, rhs, both, mean, slab_fields, pieces, direction, padded_mean, residual,
    applied, diagonal, out, halves,
):
    regressor = lax.axis_index("slab")
    planes, cells = out.shape
    columns = cells // LANES
    blocks = planes // 8
    design_k = design[0, regressor]
    scale = scale_ref[regressor]
    edge = jnp.zeros((8, cells), jnp.float32)
    for ref in (direction, padded_mean):
        ref[0:8, :] = edge
        ref[8 + planes : 16 + planes, :] = edge
    unpack_pieces(mean, padded_mean)
    depth = planes // rhs.shape[0]
    for slab in range(rhs.shape[0]):
        rows = slice(depth * slab, depth * (slab + 1))
        residual[rows, :] = rhs[slab]
        diagonal[rows, :] = both[slab, 0]
        applied[rows, :] = both[slab, 1]
    norms = []
    for block in range(blocks):
        center, sums = beside_tiles(padded_mean, block, columns)
        for t in range(columns):
            at = (slice(8 * block, 8 * block + 8), slice(LANES * t, LANES * (t + 1)))
            label = applied[at]
            kappa_field = jnp.where(
                label == 0,
                kappa[0, regressor],
                jnp.where(label == 1, kappa[1, regressor], kappa[2, regressor]),
            )
            shifted = 6.0 + kappa_field
            right_side = residual[at] + scale * (shifted * center[t] - sums[t])
            diagonal[at] = design_k * diagonal[at] + scale * shifted
            residual[at] = right_side
            direction[8 + 8 * block : 16 + 8 * block, at[1]] = right_side
            norms.append(right_side * right_side)
        norms = [sum(norms[1:], norms[0])]
    out[...] = jnp.zeros((planes, cells), jnp.float32)

    def step(iteration, norm_now):
        curvs = []
        for block in range(blocks):
            center, sums = beside_tiles(direction, block, columns)
            for t in range(columns):
                at = (slice(8 * block, 8 * block + 8), slice(LANES * t, LANES * (t + 1)))
                value = diagonal[at] * center[t] - scale * sums[t]
                applied[at] = value
                curvs.append(center[t] * value)
            curvs = [total_tile(curvs)]
        step_size = norm_now / total(curvs)
        norms = []
        for block in range(blocks):
            for t in range(columns):
                at = (slice(8 * block, 8 * block + 8), slice(LANES * t, LANES * (t + 1)))
                out[at] += step_size * direction[8 + 8 * block : 16 + 8 * block, at[1]]
                value = residual[at] - step_size * applied[at]
                residual[at] = value
                norms.append(value * value)
            norms = [total_tile(norms)]
        norm_next = total(norms)
        ratio = norm_next / norm_now
        for block in range(blocks):
            for t in range(columns):
                at = (slice(8 * block, 8 * block + 8), slice(LANES * t, LANES * (t + 1)))
                own = (slice(8 + 8 * block, 16 + 8 * block), at[1])
                direction[own] = residual[at] + ratio * direction[own]
        return norm_next

    def last(norm_now):
        curvs = []
        for block in range(blocks):
            center, sums = beside_tiles(direction, block, columns)
            for t in range(columns):
                at = (slice(8 * block, 8 * block + 8), slice(LANES * t, LANES * (t + 1)))
                curvs.append(center[t] * (diagonal[at] * center[t] - scale * sums[t]))
            curvs = [total_tile(curvs)]
        step_size = norm_now / total(curvs)
        for block in range(blocks):
            for t in range(columns):
                at = (slice(8 * block, 8 * block + 8), slice(LANES * t, LANES * (t + 1)))
                out[at] += step_size * direction[8 + 8 * block : 16 + 8 * block, at[1]]

    last(lax.fori_loop(0, ITERS - 1, step, total(norms)))
    for slab in range(rhs.shape[0]):
        slab_fields[slab] = out[depth * slab : depth * (slab + 1), :]
    pack_pieces(out, pieces, halves)


def total_tile(parts):
    while len(parts) > 1:
        parts = [
            parts[i] + parts[i + 1] if i + 1 < len(parts) else parts[i]
            for i in range(0, len(parts), 2)
        ]
    return parts[0]


def solve(design, kappa_sq, prior_scale, rhs, both, mean):
    slabs, depth, cells = rhs.shape
    planes = slabs * depth
    vmem = pl.BlockSpec(memory_space=pltpu.VMEM)
    smem = pl.BlockSpec(memory_space=pltpu.SMEM)
    field = pltpu.VMEM((planes, cells), jnp.float32)
    padded = pltpu.VMEM((planes + 16, cells), jnp.float32)
    halves = pltpu.VMEM((2, planes // 2, cells), jnp.float32)
    return pl.pallas_call(
        solve_kernel,
        out_shape=[
            jax.ShapeDtypeStruct(rhs.shape, jnp.float32),
            jax.ShapeDtypeStruct(mean.shape, jnp.float32),
        ],
        in_specs=[smem] * 3 + [vmem] * 3,
        out_specs=[vmem, vmem],
        scratch_shapes=[padded, padded, field, field, field, field, halves],
        name="solve",
    )(design, kappa_sq, prior_scale, rhs, both, mean)


def ring(axis, stride, count):
    index = lax.axis_index(axis)
    place = lax.rem(lax.div(index, stride), count)
    return axis, count - 1, lambda i: index + (lax.rem(place + i + 1, count) - place) * stride


def farthest_first(group):
    axis, peers, peer = group
    middle = (peers + 1) // 2 - 1

    def ordered(i):
        return peer(middle + lax.div(i + 1, 2) * (2 * lax.rem(i, 2) - 1))

    return axis, peers, ordered


def across(axis, low, first, count):
    index = lax.axis_index(axis)
    place = lax.rem(index, low)
    base = index - place
    other = lax.rem(base + low, 2 * low)
    return axis, count, lambda i: other + lax.rem(place + first + i, low)


def named(axis, index):
    return index if isinstance(index, dict) else {axis: index}


def turned(half, steps, low):
    slab, subject = lax.axis_index("slab"), lax.axis_index("subj")
    y_lo = lax.rem(subject, ROW)
    y = lax.rem(lax.div(slab, half) * ROW + y_lo + steps, 2 * ROW)
    return {"subj": subject - y_lo + lax.rem(y, ROW), "slab": lax.div(y, ROW) * half + low}


def detour(source, target, passing, sems):
    half = source.shape[0] // 2
    count = passing.shape[0]
    first = half - count
    back, on = 3 * ROW // 2, ROW // 2
    slab = lax.axis_index("slab")
    place = lax.rem(slab, half)
    base = lax.rem(slab - place + half, 2 * half)

    def low(i):
        return lax.rem(place + first + i, half)

    out = Exchange(
        (None, count, lambda i: turned(half, back, place)),
        lambda i, to: source.at[base + low(i)],
        lambda i: passing.at[i],
        sems[0:2],
    )
    origin = turned(half, on, place)["slab"]
    onward = Exchange(
        (None, count, lambda i: turned(half, back, low(i))),
        lambda i, to: passing.at[i],
        lambda i: target.at[origin],
        sems[2:4],
    )
    groups = [(None, half, lambda i, k=k: turned(half, k, i)) for k in (back, on)]
    return out, onward, groups


def greet(*groups):
    barrier = pltpu.get_barrier_semaphore()
    for axis, count, peer in groups:

        def signal(i, carry):
            pl.semaphore_signal(
                barrier, inc=1, device_id=named(axis, peer(i)), device_id_type=pl.DeviceIdType.MESH
            )
            return carry

        lax.fori_loop(0, count, signal, 0)
    pl.semaphore_wait(barrier, sum(count for _, count, _ in groups))


class Exchange:
    def __init__(self, group, source, target, sems):
        self.axis, self.count, self.peer = group
        self.source, self.target = source, target
        self.send, self.receive = sems

    def remote(self, i):
        to = self.peer(i)
        return pltpu.make_async_remote_copy(
            src_ref=self.source(i, to),
            dst_ref=self.target(i),
            send_sem=self.send.at[i],
            recv_sem=self.receive.at[i],
            device_id=named(self.axis, to),
            device_id_type=pl.DeviceIdType.MESH,
        )

    def start(self):
        def one(i, carry):
            self.remote(i).start()
            return carry

        lax.fori_loop(0, self.count, one, 0)

    def wait(self):
        def one(i, carry):
            self.remote(i).wait()
            return carry

        lax.fori_loop(0, self.count, one, 0)


def exchange_sems(*counts):
    return [pltpu.SemaphoreType.DMA((count,)) for count in counts for _ in range(2)]


def bring_kernel(rhs, both, mean, rhs_out, both_out, mean_out, held, passing, own, *sems):
    slabs, subjects = rhs.shape[0], mean_out.shape[0]
    slab, subject = lax.axis_index("slab"), lax.axis_index("subj")
    half = slabs // 2
    mirror = lax.rem(slab + half, slabs)
    core = lax.rem(slab, CORES)
    near = ring("slab", 1, half)
    far = across("slab", half, 0, half)
    early = across("slab", half, 0, half // 2)
    along_x = ring("slab", CORES, half // CORES)
    along_y = ring("subj", 1, ROW)
    depth = subjects // ROW
    along_z = ring("subj", ROW, depth)
    up, down = depth // 2, depth - 1 - depth // 2
    above, below = along_z[2](0), along_z[2](depth - 2)
    z = lax.div(subject, ROW)
    partner = ring("slab", 1, CORES)[2](0)

    def pair(k):
        return sems[2 * k], sems[2 * k + 1]

    def take(ref):
        return lambda i, to: ref.at[to]

    def put(ref, index):
        return lambda i: ref.at[index]

    small_near = Exchange(near, take(mean), put(held, slab), pair(0))
    small_far = Exchange(far, take(mean), put(held, slab), pair(1))
    large_near = Exchange(near, take(rhs), put(rhs_out, slab), pair(2))
    large_early = Exchange(early, take(rhs), put(rhs_out, slab), pair(3))
    out, last, around = detour(rhs, rhs_out, passing, sems[-4:])
    over = Exchange(
        ("slab", 1, lambda i: mirror), lambda i, to: both, put(both_out, slab), pair(4)
    )
    beside = Exchange(along_x, lambda i, to: both, put(both_out, slab), pair(5))
    passed = Exchange(
        along_x, lambda i, to: both_out.at[mirror], put(both_out, mirror), pair(6)
    )
    twin = Exchange(
        ("slab", half, lambda i: partner),
        lambda i, to: both_out.at[CORES * i + core],
        lambda i: both_out.at[CORES * i + core],
        pair(7),
    )
    row = Exchange(along_y, lambda i, to: held, put(mean_out, subject), pair(8))

    def hop(to, distance, k):
        layer = mean_out.at[pl.ds(ROW * lax.rem(z + depth + distance, depth), ROW)]
        return Exchange(("subj", 1, lambda i: to), lambda i, _: layer, lambda i: layer, pair(k))

    ups = [hop(above, -step, 9 + step) for step in range(up)]
    downs = [hop(below, step, 9 + up + step) for step in range(down)]

    def onward(step):
        for hops in (ups, downs):
            if step < len(hops):
                hops[step - 1].wait()
                hops[step].start()

    kept = [
        pltpu.make_async_copy(mean.at[slab], held.at[slab], own.at[0]),
        pltpu.make_async_copy(rhs.at[slab], rhs_out.at[slab], own.at[1]),
        pltpu.make_async_copy(both, both_out.at[slab], own.at[2]),
        pltpu.make_async_copy(held, mean_out.at[subject], own.at[3]),
    ]
    greet(near, far, along_y, along_z, *around)
    small_far.start()
    small_near.start()
    over.start()
    beside.start()
    out.start()
    large_early.start()
    large_near.start()
    for copy in kept[:3]:
        copy.start()
    kept[0].wait()
    small_near.wait()
    small_far.wait()
    row.start()
    kept[3].start()
    over.wait()
    passed.start()
    kept[3].wait()
    row.wait()
    ups[0].start()
    downs[0].start()
    onward(1)
    kept[2].wait()
    beside.wait()
    passed.wait()
    twin.start()
    out.wait()
    last.start()
    for step in range(2, max(up, down)):
        onward(step)
    kept[1].wait()
    large_near.wait()
    twin.wait()
    large_early.wait()
    last.wait()
    ups[-1].wait()
    downs[-1].wait()


def bring(rhs, both, mean):
    slabs, subjects = lax.axis_size("slab"), lax.axis_size("subj")
    half = slabs // 2
    x_peers = half // CORES - 1
    vmem = pl.BlockSpec(memory_space=pltpu.VMEM)
    return pl.pallas_call(
        bring_kernel,
        out_shape=[
            jax.ShapeDtypeStruct(rhs.shape, jnp.float32),
            jax.ShapeDtypeStruct((slabs,) + both.shape, jnp.float32),
            jax.ShapeDtypeStruct((subjects,) + mean.shape, jnp.float32),
        ],
        in_specs=[vmem] * 3,
        out_specs=[vmem] * 3,
        scratch_shapes=[
            pltpu.VMEM(mean.shape, jnp.float32),
            pltpu.VMEM((half // 2,) + rhs.shape[1:], jnp.float32),
            pltpu.SemaphoreType.DMA((4,)),
            *exchange_sems(half - 1, half, half - 1, half // 2, 1, x_peers, x_peers, half),
            *exchange_sems(ROW - 1, *[1] * (subjects // ROW - 1), half // 2, half // 2),
        ],
        compiler_params=pltpu.CompilerParams(collective_id=0, has_side_effects=True),
        name="bring",
    )(rhs, both, mean)


def give_kernel(
    fields, pieces, fields_out, mean_out, layers, partial, rows, summed, passing, own, *sems
):
    slabs, subjects = fields.shape[0], pieces.shape[0]
    slab, subject = lax.axis_index("slab"), lax.axis_index("subj")
    half = slabs // 2
    y = lax.rem(subject, ROW)
    z = lax.div(subject, ROW)
    near = ring("slab", 1, half)
    far = across("slab", half, 0, half)
    along_y = ring("subj", 1, ROW)
    along_z = farthest_first(ring("subj", ROW, subjects // ROW))

    def pair(k):
        return sems[2 * k], sems[2 * k + 1]

    def take(ref):
        return lambda i, to: ref.at[to]

    def put(ref, index):
        return lambda i: ref.at[index]

    column = Exchange(
        along_z, lambda i, to: pieces.at[pl.ds(to - y, ROW)], put(layers, z), pair(0)
    )
    row = Exchange(
        along_y, lambda i, to: partial.at[lax.rem(to, ROW)], put(rows, y), pair(1)
    )
    early = across("slab", half, 0, half // 2)
    large_far = Exchange(early, take(fields), put(fields_out, slab), pair(2))
    out, last, around = detour(fields, fields_out, passing, sems[-4:])
    large_near = Exchange(near, take(fields), put(fields_out, slab), pair(3))
    small_far = Exchange(far, take(summed), put(mean_out, slab), pair(4))
    small_near = Exchange(near, take(summed), put(mean_out, slab), pair(5))
    kept = [
        pltpu.make_async_copy(pieces.at[pl.ds(subject - y, ROW)], layers.at[z], own.at[0]),
        pltpu.make_async_copy(partial.at[y], rows.at[y], own.at[1]),
        pltpu.make_async_copy(fields.at[slab], fields_out.at[slab], own.at[2]),
        pltpu.make_async_copy(summed.at[slab], mean_out.at[slab], own.at[3]),
    ]
    greet(near, far, along_y, along_z, *around)
    column.start()
    out.start()
    large_far.start()
    large_near.start()
    kept[0].start()
    kept[2].start()
    kept[0].wait()
    out.wait()
    last.start()
    column.wait()
    partial[...] = jnp.sum(layers[...], axis=0)
    row.start()
    kept[1].start()
    kept[1].wait()
    row.wait()
    summed[...] = jnp.sum(rows[...], axis=0)
    small_far.start()
    small_near.start()
    kept[3].start()
    for copy in kept[2:]:
        copy.wait()
    for exchange in (large_near, large_far, last, small_near, small_far):
        exchange.wait()


def give(fields, pieces):
    slabs, subjects = lax.axis_size("slab"), lax.axis_size("subj")
    half, depth = slabs // 2, subjects // ROW
    vmem = pl.BlockSpec(memory_space=pltpu.VMEM)
    small = pieces.shape[1:]
    return pl.pallas_call(
        give_kernel,
        out_shape=[
            jax.ShapeDtypeStruct(fields.shape, jnp.float32),
            jax.ShapeDtypeStruct(small, jnp.float32),
        ],
        in_specs=[vmem] * 2,
        out_specs=[vmem] * 2,
        scratch_shapes=[
            pltpu.VMEM((depth, ROW) + small, jnp.float32),
            pltpu.VMEM((ROW,) + small, jnp.float32),
            pltpu.VMEM((ROW,) + small, jnp.float32),
            pltpu.VMEM(small, jnp.float32),
            pltpu.VMEM((half // 2,) + fields.shape[1:], jnp.float32),
            pltpu.SemaphoreType.DMA((4,)),
            *exchange_sems(depth - 1, ROW - 1, half // 2, half - 1, half, half - 1),
            *exchange_sems(half // 2, half // 2),
        ],
        compiler_params=pltpu.CompilerParams(collective_id=1, has_side_effects=True),
        name="give",
    )(fields, pieces)


def local(
    data_rhs,
    inv_var,
    design,
    keep_mask,
    brain_mask,
    tissue,
    kappa_sq,
    prior_scale,
    mean_field,
    pop_noise,
):
    slabs, subjects = lax.axis_size("slab"), lax.axis_size("subj")
    depth, cells = tissue.shape
    width = cells // subjects
    pair = depth // 2
    spare = jnp.zeros((slabs, pair, LANES - 2 * width), jnp.float32)
    mean = jnp.concatenate([mean_field[:, :pair], mean_field[:, pair:], spare], axis=2)
    factor = inv_var[0] * (brain_mask.astype(jnp.float32) * keep_mask[0].astype(jnp.float32))
    both = jnp.stack([factor, tissue.astype(jnp.float32)])
    rhs, both, mean = bring(data_rhs[0], both, mean)
    mean = mean.reshape(subjects, slabs * pair, LANES)
    fields, pieces = solve(design, kappa_sq, prior_scale, rhs, both, mean)
    back, summed = give(fields, pieces.reshape(subjects, slabs, pair, LANES))
    summed = jnp.concatenate([summed[..., :width], summed[..., width : 2 * width]], axis=1)
    divisor = subjects + MEAN_PRECISION
    new_mean = summed / divisor + pop_noise / math.sqrt(divisor)
    return (back[None], new_mean)


def solution(mesh):
    in_specs = (
        P("subj", None, "slab", None),
        P("subj", "slab", None),
        P("subj", None),
        P("subj", "slab", None),
        P("slab", None),
        P("slab", None),
        P(),
        P(),
        P(None, "slab", "subj"),
        P(None, "slab", "subj"),
    )
    out_specs = (P("subj", None, "slab", None), P(None, "slab", "subj"))
    return jax.shard_map(local, mesh=mesh, in_specs=in_specs, out_specs=out_specs, check_vma=False)
```

```python
import math

import jax
import jax.numpy as jnp
from jax import lax
from jax.experimental import pallas as pl
from jax.experimental.pallas import tpu as pltpu
from jax.sharding import PartitionSpec as P

ITERS = 8
CX = 64
LANES = 128
MEAN_PRECISION = 1.0
CORES = 2
ROW = 4


def tiles_of(ref, row, columns):
    return [ref[row : row + 8, LANES * t : LANES * (t + 1)] for t in range(columns)]


def beside_tiles(ref, block, columns):
    lane = lax.broadcasted_iota(jnp.int32, (8, LANES), 1)
    column = lane % CX
    has_left = column > 0
    has_right = column < CX - 1
    low = lane < CX
    row = 8 + 8 * block
    center = tiles_of(ref, row, columns)
    before = tiles_of(ref, row - 1, columns)
    after = tiles_of(ref, row + 1, columns)
    swapped = [pltpu.roll(tile, CX, 1) for tile in center]
    zero = jnp.zeros((8, LANES), jnp.float32)
    sums = []
    for t in range(columns):
        left = jnp.where(has_left, pltpu.roll(center[t], 1, 1), 0.0)
        right = jnp.where(has_right, pltpu.roll(center[t], LANES - 1, 1), 0.0)
        prev_half = swapped[t - 1] if t else zero
        next_half = swapped[t + 1] if t + 1 < columns else zero
        rows = swapped[t] + jnp.where(low, prev_half, next_half)
        sums.append((left + right) + rows + (before[t] + after[t]))
    return center, sums


def total(parts):
    while len(parts) > 1:
        parts = [
            parts[i] + parts[i + 1] if i + 1 < len(parts) else parts[i]
            for i in range(0, len(parts), 2)
        ]
    return jnp.sum(parts[0], axis=(0, 1), keepdims=True)


def unpack_pieces(pieces, padded):
    count, half, _ = pieces.shape
    cells = padded.shape[1]
    width = cells // count
    lane = lax.broadcasted_iota(jnp.int32, (half, LANES), 1)
    for upper in range(2):
        for t in range(cells // LANES):
            value = None
            first = LANES * t // width
            for piece in range(first, (LANES * (t + 1) - 1) // width + 1):
                start = piece * width - LANES * t
                moved = pieces[piece]
                turn = (start - upper * width) % LANES
                if turn:
                    moved = pltpu.roll(moved, turn, 1)
                value = moved if value is None else jnp.where(lane >= start, moved, value)
            for pair in range(half // 2):
                row = 8 + 4 * pair + 2 * upper
                padded[row : row + 2, LANES * t : LANES * (t + 1)] = value[2 * pair : 2 * pair + 2]


def pack_pieces(fields, pieces, halves):
    count, half, _ = pieces.shape
    cells = fields.shape[1]
    width = cells // count
    lane = lax.broadcasted_iota(jnp.int32, (half, LANES), 1)
    for upper in range(2):
        for pair in range(half // 2):
            row = 4 * pair + 2 * upper
            halves[upper, 2 * pair : 2 * pair + 2, :] = fields[row : row + 2, :]
    for piece in range(count):
        t, offset = divmod(piece * width, LANES)
        sides = []
        for upper in range(2):
            turn = (upper * width - offset) % LANES
            value = None
            for source in range(t, (piece * width + width - 1) // LANES + 1):
                tile = halves[upper, :, LANES * source : LANES * (source + 1)]
                moved = pltpu.roll(tile, turn, 1) if turn else tile
                if value is None:
                    value = moved
                else:
                    value = jnp.where(lane < LANES - offset + upper * width, value, moved)
            sides.append(value)
        pieces[piece] = jnp.where(lane < width, sides[0], sides[1])


def solve_kernel(
    design, kappa, scale_ref, rhs, both, mean, slab_fields, pieces, direction, padded_mean, residual,
    applied, diagonal, out, halves,
):
    regressor = lax.axis_index("slab")
    planes, cells = out.shape
    columns = cells // LANES
    blocks = planes // 8
    design_k = design[0, regressor]
    scale = scale_ref[regressor]
    edge = jnp.zeros((8, cells), jnp.float32)
    for ref in (direction, padded_mean):
        ref[0:8, :] = edge
        ref[8 + planes : 16 + planes, :] = edge
    unpack_pieces(mean, padded_mean)
    depth = planes // rhs.shape[0]
    for slab in range(rhs.shape[0]):
        rows = slice(depth * slab, depth * (slab + 1))
        residual[rows, :] = rhs[slab]
        diagonal[rows, :] = both[slab, 0]
        applied[rows, :] = both[slab, 1]
    norms = []
    for block in range(blocks):
        center, sums = beside_tiles(padded_mean, block, columns)
        for t in range(columns):
            at = (slice(8 * block, 8 * block + 8), slice(LANES * t, LANES * (t + 1)))
            label = applied[at]
            kappa_field = jnp.where(
                label == 0,
                kappa[0, regressor],
                jnp.where(label == 1, kappa[1, regressor], kappa[2, regressor]),
            )
            shifted = 6.0 + kappa_field
            right_side = residual[at] + scale * (shifted * center[t] - sums[t])
            diagonal[at] = design_k * diagonal[at] + scale * shifted
            residual[at] = right_side
            direction[8 + 8 * block : 16 + 8 * block, at[1]] = right_side
            norms.append(right_side * right_side)
        norms = [sum(norms[1:], norms[0])]
    out[...] = jnp.zeros((planes, cells), jnp.float32)

    def step(iteration, norm_now):
        curvs = []
        for block in range(blocks):
            center, sums = beside_tiles(direction, block, columns)
            for t in range(columns):
                at = (slice(8 * block, 8 * block + 8), slice(LANES * t, LANES * (t + 1)))
                value = diagonal[at] * center[t] - scale * sums[t]
                applied[at] = value
                curvs.append(center[t] * value)
            curvs = [total_tile(curvs)]
        step_size = norm_now / total(curvs)
        norms = []
        for block in range(blocks):
            for t in range(columns):
                at = (slice(8 * block, 8 * block + 8), slice(LANES * t, LANES * (t + 1)))
                out[at] += step_size * direction[8 + 8 * block : 16 + 8 * block, at[1]]
                value = residual[at] - step_size * applied[at]
                residual[at] = value
                norms.append(value * value)
            norms = [total_tile(norms)]
        norm_next = total(norms)
        ratio = norm_next / norm_now
        for block in range(blocks):
            for t in range(columns):
                at = (slice(8 * block, 8 * block + 8), slice(LANES * t, LANES * (t + 1)))
                own = (slice(8 + 8 * block, 16 + 8 * block), at[1])
                direction[own] = residual[at] + ratio * direction[own]
        return norm_next

    def last(norm_now):
        curvs = []
        for block in range(blocks):
            center, sums = beside_tiles(direction, block, columns)
            for t in range(columns):
                at = (slice(8 * block, 8 * block + 8), slice(LANES * t, LANES * (t + 1)))
                curvs.append(center[t] * (diagonal[at] * center[t] - scale * sums[t]))
            curvs = [total_tile(curvs)]
        step_size = norm_now / total(curvs)
        for block in range(blocks):
            for t in range(columns):
                at = (slice(8 * block, 8 * block + 8), slice(LANES * t, LANES * (t + 1)))
                out[at] += step_size * direction[8 + 8 * block : 16 + 8 * block, at[1]]

    last(lax.fori_loop(0, ITERS - 1, step, total(norms)))
    for slab in range(rhs.shape[0]):
        slab_fields[slab] = out[depth * slab : depth * (slab + 1), :]
    pack_pieces(out, pieces, halves)


def total_tile(parts):
    while len(parts) > 1:
        parts = [
            parts[i] + parts[i + 1] if i + 1 < len(parts) else parts[i]
            for i in range(0, len(parts), 2)
        ]
    return parts[0]


def solve(design, kappa_sq, prior_scale, rhs, both, mean):
    slabs, depth, cells = rhs.shape
    planes = slabs * depth
    vmem = pl.BlockSpec(memory_space=pltpu.VMEM)
    smem = pl.BlockSpec(memory_space=pltpu.SMEM)
    field = pltpu.VMEM((planes, cells), jnp.float32)
    padded = pltpu.VMEM((planes + 16, cells), jnp.float32)
    halves = pltpu.VMEM((2, planes // 2, cells), jnp.float32)
    return pl.pallas_call(
        solve_kernel,
        out_shape=[
            jax.ShapeDtypeStruct(rhs.shape, jnp.float32),
            jax.ShapeDtypeStruct(mean.shape, jnp.float32),
        ],
        in_specs=[smem] * 3 + [vmem] * 3,
        out_specs=[vmem, vmem],
        scratch_shapes=[padded, padded, field, field, field, field, halves],
        name="solve",
    )(design, kappa_sq, prior_scale, rhs, both, mean)


def ring(axis, stride, count):
    index = lax.axis_index(axis)
    place = lax.rem(lax.div(index, stride), count)
    return axis, count - 1, lambda i: index + (lax.rem(place + i + 1, count) - place) * stride


def farthest_first(group):
    axis, peers, peer = group
    middle = (peers + 1) // 2 - 1

    def ordered(i):
        return peer(middle + lax.div(i + 1, 2) * (2 * lax.rem(i, 2) - 1))

    return axis, peers, ordered


def across(axis, low, first, count):
    index = lax.axis_index(axis)
    place = lax.rem(index, low)
    base = index - place
    other = lax.rem(base + low, 2 * low)
    return axis, count, lambda i: other + lax.rem(place + first + i, low)


def named(axis, index):
    return index if isinstance(index, dict) else {axis: index}


def turned(half, steps, low):
    slab, subject = lax.axis_index("slab"), lax.axis_index("subj")
    y_lo = lax.rem(subject, ROW)
    y = lax.rem(lax.div(slab, half) * ROW + y_lo + steps, 2 * ROW)
    return {"subj": subject - y_lo + lax.rem(y, ROW), "slab": lax.div(y, ROW) * half + low}


def detour(source, target, passing, sems):
    half = source.shape[0] // 2
    count = passing.shape[0]
    first = half - count
    back, on = 3 * ROW // 2, ROW // 2
    slab = lax.axis_index("slab")
    place = lax.rem(slab, half)
    base = lax.rem(slab - place + half, 2 * half)

    def low(i):
        return lax.rem(place + first + i, half)

    out = Exchange(
        (None, count, lambda i: turned(half, back, place)),
        lambda i, to: source.at[base + low(i)],
        lambda i: passing.at[i],
        sems[0:2],
    )
    origin = turned(half, on, place)["slab"]
    onward = Exchange(
        (None, count, lambda i: turned(half, back, low(i))),
        lambda i, to: passing.at[i],
        lambda i: target.at[origin],
        sems[2:4],
    )
    groups = [(None, half, lambda i, k=k: turned(half, k, i)) for k in (back, on)]
    return out, onward, groups


def greet(*groups):
    barrier = pltpu.get_barrier_semaphore()
    for axis, count, peer in groups:

        def signal(i, carry):
            pl.semaphore_signal(
                barrier, inc=1, device_id=named(axis, peer(i)), device_id_type=pl.DeviceIdType.MESH
            )
            return carry

        lax.fori_loop(0, count, signal, 0)
    pl.semaphore_wait(barrier, sum(count for _, count, _ in groups))


class Exchange:
    def __init__(self, group, source, target, sems):
        self.axis, self.count, self.peer = group
        self.source, self.target = source, target
        self.send, self.receive = sems

    def remote(self, i):
        to = self.peer(i)
        return pltpu.make_async_remote_copy(
            src_ref=self.source(i, to),
            dst_ref=self.target(i),
            send_sem=self.send.at[i],
            recv_sem=self.receive.at[i],
            device_id=named(self.axis, to),
            device_id_type=pl.DeviceIdType.MESH,
        )

    def start(self):
        def one(i, carry):
            self.remote(i).start()
            return carry

        lax.fori_loop(0, self.count, one, 0)

    def wait(self):
        def one(i, carry):
            self.remote(i).wait()
            return carry

        lax.fori_loop(0, self.count, one, 0)


def exchange_sems(*counts):
    return [pltpu.SemaphoreType.DMA((count,)) for count in counts for _ in range(2)]


def bring_kernel(rhs, both, mean, rhs_out, both_out, mean_out, held, passing, own, *sems):
    slabs, subjects = rhs.shape[0], mean_out.shape[0]
    slab, subject = lax.axis_index("slab"), lax.axis_index("subj")
    half = slabs // 2
    mirror = lax.rem(slab + half, slabs)
    core = lax.rem(slab, CORES)
    near = ring("slab", 1, half)
    far = across("slab", half, 0, half)
    early = across("slab", half, 0, half // 2)
    along_x = ring("slab", CORES, half // CORES)
    along_y = ring("subj", 1, ROW)
    depth = subjects // ROW
    along_z = ring("subj", ROW, depth)
    up, down = depth // 2, depth - 1 - depth // 2
    above, below = along_z[2](0), along_z[2](depth - 2)
    z = lax.div(subject, ROW)
    partner = ring("slab", 1, CORES)[2](0)

    def pair(k):
        return sems[2 * k], sems[2 * k + 1]

    def take(ref):
        return lambda i, to: ref.at[to]

    def put(ref, index):
        return lambda i: ref.at[index]

    small_near = Exchange(near, take(mean), put(held, slab), pair(0))
    small_far = Exchange(far, take(mean), put(held, slab), pair(1))
    large_near = Exchange(near, take(rhs), put(rhs_out, slab), pair(2))
    large_early = Exchange(early, take(rhs), put(rhs_out, slab), pair(3))
    out, last, around = detour(rhs, rhs_out, passing, sems[-4:])
    over = Exchange(
        ("slab", 1, lambda i: mirror), lambda i, to: both, put(both_out, slab), pair(4)
    )
    beside = Exchange(along_x, lambda i, to: both, put(both_out, slab), pair(5))
    passed = Exchange(
        along_x, lambda i, to: both_out.at[mirror], put(both_out, mirror), pair(6)
    )
    twin = Exchange(
        ("slab", half, lambda i: partner),
        lambda i, to: both_out.at[CORES * i + core],
        lambda i: both_out.at[CORES * i + core],
        pair(7),
    )
    row = Exchange(along_y, lambda i, to: held, put(mean_out, subject), pair(8))

    def hop(to, distance, k):
        layer = mean_out.at[pl.ds(ROW * lax.rem(z + depth + distance, depth), ROW)]
        return Exchange(("subj", 1, lambda i: to), lambda i, _: layer, lambda i: layer, pair(k))

    ups = [hop(above, -step, 9 + step) for step in range(up)]
    downs = [hop(below, step, 9 + up + step) for step in range(down)]

    def onward(step):
        for hops in (ups, downs):
            if step < len(hops):
                hops[step - 1].wait()
                hops[step].start()

    kept = [
        pltpu.make_async_copy(mean.at[slab], held.at[slab], own.at[0]),
        pltpu.make_async_copy(rhs.at[slab], rhs_out.at[slab], own.at[1]),
        pltpu.make_async_copy(both, both_out.at[slab], own.at[2]),
        pltpu.make_async_copy(held, mean_out.at[subject], own.at[3]),
    ]
    greet(near, far, along_y, along_z, *around)
    small_far.start()
    small_near.start()
    over.start()
    beside.start()
    out.start()
    large_early.start()
    large_near.start()
    for copy in kept[:3]:
        copy.start()
    kept[0].wait()
    small_near.wait()
    small_far.wait()
    row.start()
    kept[3].start()
    out.wait()
    last.start()
    over.wait()
    passed.start()
    kept[3].wait()
    row.wait()
    ups[0].start()
    downs[0].start()
    onward(1)
    kept[2].wait()
    beside.wait()
    passed.wait()
    twin.start()
    for step in range(2, max(up, down)):
        onward(step)
    kept[1].wait()
    large_near.wait()
    twin.wait()
    large_early.wait()
    last.wait()
    ups[-1].wait()
    downs[-1].wait()


def bring(rhs, both, mean):
    slabs, subjects = lax.axis_size("slab"), lax.axis_size("subj")
    half = slabs // 2
    x_peers = half // CORES - 1
    vmem = pl.BlockSpec(memory_space=pltpu.VMEM)
    return pl.pallas_call(
        bring_kernel,
        out_shape=[
            jax.ShapeDtypeStruct(rhs.shape, jnp.float32),
            jax.ShapeDtypeStruct((slabs,) + both.shape, jnp.float32),
            jax.ShapeDtypeStruct((subjects,) + mean.shape, jnp.float32),
        ],
        in_specs=[vmem] * 3,
        out_specs=[vmem] * 3,
        scratch_shapes=[
            pltpu.VMEM(mean.shape, jnp.float32),
            pltpu.VMEM((half // 2,) + rhs.shape[1:], jnp.float32),
            pltpu.SemaphoreType.DMA((4,)),
            *exchange_sems(half - 1, half, half - 1, half // 2, 1, x_peers, x_peers, half),
            *exchange_sems(ROW - 1, *[1] * (subjects // ROW - 1), half // 2, half // 2),
        ],
        compiler_params=pltpu.CompilerParams(collective_id=0, has_side_effects=True),
        name="bring",
    )(rhs, both, mean)


def give_kernel(
    fields, pieces, fields_out, mean_out, layers, partial, rows, summed, passing, own, *sems
):
    slabs, subjects = fields.shape[0], pieces.shape[0]
    slab, subject = lax.axis_index("slab"), lax.axis_index("subj")
    half = slabs // 2
    y = lax.rem(subject, ROW)
    z = lax.div(subject, ROW)
    near = ring("slab", 1, half)
    far = across("slab", half, 0, half)
    along_y = ring("subj", 1, ROW)
    along_z = farthest_first(ring("subj", ROW, subjects // ROW))

    def pair(k):
        return sems[2 * k], sems[2 * k + 1]

    def take(ref):
        return lambda i, to: ref.at[to]

    def put(ref, index):
        return lambda i: ref.at[index]

    column = Exchange(
        along_z, lambda i, to: pieces.at[pl.ds(to - y, ROW)], put(layers, z), pair(0)
    )
    row = Exchange(
        along_y, lambda i, to: partial.at[lax.rem(to, ROW)], put(rows, y), pair(1)
    )
    early = across("slab", half, 0, half // 2)
    large_far = Exchange(early, take(fields), put(fields_out, slab), pair(2))
    out, last, around = detour(fields, fields_out, passing, sems[-4:])
    large_near = Exchange(near, take(fields), put(fields_out, slab), pair(3))
    small_far = Exchange(far, take(summed), put(mean_out, slab), pair(4))
    small_near = Exchange(near, take(summed), put(mean_out, slab), pair(5))
    kept = [
        pltpu.make_async_copy(pieces.at[pl.ds(subject - y, ROW)], layers.at[z], own.at[0]),
        pltpu.make_async_copy(partial.at[y], rows.at[y], own.at[1]),
        pltpu.make_async_copy(fields.at[slab], fields_out.at[slab], own.at[2]),
        pltpu.make_async_copy(summed.at[slab], mean_out.at[slab], own.at[3]),
    ]
    greet(near, far, along_y, along_z, *around)
    column.start()
    out.start()
    large_far.start()
    large_near.start()
    kept[0].start()
    kept[2].start()
    kept[0].wait()
    out.wait()
    last.start()
    column.wait()
    partial[...] = jnp.sum(layers[...], axis=0)
    row.start()
    kept[1].start()
    kept[1].wait()
    row.wait()
    summed[...] = jnp.sum(rows[...], axis=0)
    small_far.start()
    small_near.start()
    kept[3].start()
    for copy in kept[2:]:
        copy.wait()
    for exchange in (large_near, large_far, last, small_near, small_far):
        exchange.wait()


def give(fields, pieces):
    slabs, subjects = lax.axis_size("slab"), lax.axis_size("subj")
    half, depth = slabs // 2, subjects // ROW
    vmem = pl.BlockSpec(memory_space=pltpu.VMEM)
    small = pieces.shape[1:]
    return pl.pallas_call(
        give_kernel,
        out_shape=[
            jax.ShapeDtypeStruct(fields.shape, jnp.float32),
            jax.ShapeDtypeStruct(small, jnp.float32),
        ],
        in_specs=[vmem] * 2,
        out_specs=[vmem] * 2,
        scratch_shapes=[
            pltpu.VMEM((depth, ROW) + small, jnp.float32),
            pltpu.VMEM((ROW,) + small, jnp.float32),
            pltpu.VMEM((ROW,) + small, jnp.float32),
            pltpu.VMEM(small, jnp.float32),
            pltpu.VMEM((half // 2,) + fields.shape[1:], jnp.float32),
            pltpu.SemaphoreType.DMA((4,)),
            *exchange_sems(depth - 1, ROW - 1, half // 2, half - 1, half, half - 1),
            *exchange_sems(half // 2, half // 2),
        ],
        compiler_params=pltpu.CompilerParams(collective_id=1, has_side_effects=True),
        name="give",
    )(fields, pieces)


def local(
    data_rhs,
    inv_var,
    design,
    keep_mask,
    brain_mask,
    tissue,
    kappa_sq,
    prior_scale,
    mean_field,
    pop_noise,
):
    slabs, subjects = lax.axis_size("slab"), lax.axis_size("subj")
    depth, cells = tissue.shape
    width = cells // subjects
    pair = depth // 2
    spare = jnp.zeros((slabs, pair, LANES - 2 * width), jnp.float32)
    mean = jnp.concatenate([mean_field[:, :pair], mean_field[:, pair:], spare], axis=2)
    factor = inv_var[0] * (brain_mask.astype(jnp.float32) * keep_mask[0].astype(jnp.float32))
    both = jnp.stack([factor, tissue.astype(jnp.float32)])
    rhs, both, mean = bring(data_rhs[0], both, mean)
    mean = mean.reshape(subjects, slabs * pair, LANES)
    fields, pieces = solve(design, kappa_sq, prior_scale, rhs, both, mean)
    back, summed = give(fields, pieces.reshape(subjects, slabs, pair, LANES))
    summed = jnp.concatenate([summed[..., :width], summed[..., width : 2 * width]], axis=1)
    divisor = subjects + MEAN_PRECISION
    new_mean = summed / divisor + pop_noise / math.sqrt(divisor)
    return (back[None], new_mean)


def solution(mesh):
    in_specs = (
        P("subj", None, "slab", None),
        P("subj", "slab", None),
        P("subj", None),
        P("subj", "slab", None),
        P("slab", None),
        P("slab", None),
        P(),
        P(),
        P(None, "slab", "subj"),
        P(None, "slab", "subj"),
    )
    out_specs = (P("subj", None, "slab", None), P(None, "slab", "subj"))
    return jax.shard_map(local, mesh=mesh, in_specs=in_specs, out_specs=out_specs, check_vma=False)
```
